256 devices in a mesh: blk: 128 (over x_lo, z, y, core), rep: 2 (over x_hi).
Axes of the slice: x: 4 (x_hi: 2, x_lo: 2; x = x_hi * 2 + x_lo), y: 4, z: 8, core: 2. Of those that a mesh axis runs over, the one named last changes fastest.
Arguments:
- factors: float32 [128, 2, 300, 512], P('blk', None, 'rep'), may hold values from -1.5 to 1.5
- state: float32 [128, 2, 300, 512], P('blk', None, 'rep'), may hold values from 30 to 3000
- counts: int32 [128, 8, 512, 512], P('blk'), may hold values from 0 to 1024, as said below
Outputs:
- step: float32 [128, 2, 300, 512], P('blk', None, 'rep')
- new_state: float32 [128, 2, 300, 512], P('blk', None, 'rep')
The draws below stay inside these ranges and needn't reach their ends.
Inputs may be any that keep to these rules, and one draw needn't show every extreme that they name: counts[p, r] is the tile of the two blocks that meet at player p in round r, and each pair of blocks meets at most once in the 8 rounds.
All inputs are finite; a program needn't handle non-finite values.
Results may differ from the reference program's by a relative error of at most 0.0003.
Values sent between devices are 32-bit elements; how exact they have to be, the bound alone decides.
A program may use at most 128 MiB of HBM per device.

```python
import math
import jax
import jax.numpy as jnp
from jax import lax

B = 512
D = 300
ROUNDS = 8
PLAYERS = 128


def draw_counts(key, part):
    first, second, third = jax.random.split(jax.random.fold_in(key, 17), 3)
    shape = (PLAYERS, ROUNDS, B, B)
    mantissa = jax.random.randint(first, shape, 0, 1024)
    shifted = jax.random.randint(second, shape, 0, 10)
    present = jax.random.randint(third, shape, 0, 3)
    value = 1 + jnp.right_shift(mantissa, shifted)
    return jnp.where(present == 0, 0, value).astype(jnp.int32)


def block_scale(stream_key, dims, shards, low, high):
    gain, own = 1.0, jax.random.fold_in(stream_key, 6)
    for axis_at, blocks in shards:
        heights = jnp.exp(jax.random.uniform(jax.random.fold_in(own, axis_at), (blocks,), jnp.float32, low / len(shards), high / len(shards)))
        gain = gain * jnp.repeat(heights, dims[axis_at] // blocks).reshape([-1 if axis == axis_at else 1 for axis in range(len(dims))])
    return gain


def normal_values(own_key, dims, scale, most, cuts=(), kind=jnp.bfloat16):
    result = jax.random.normal(own_key, dims, jnp.float32) * scale
    if len(cuts) > 0:
        result = block_scale(own_key, dims, cuts, -0.22, 0.18) * result
    return jnp.clip(result, min=-most, max=most).astype(kind)


def setup_inputs(seed: int = 0) -> dict:
    keys = jax.random.split(jax.random.key(seed), 4)
    factors = normal_values(keys[0], (PLAYERS, 2, D, B), 0.25, 1.5, ((0, 128), (2, 2)), jnp.float32)
    state = jnp.clip(jnp.exp(math.log(3000.0) - 4.6051702 * jax.random.uniform(keys[1], (PLAYERS, 2, D, B), jnp.float32) ** block_scale(keys[1], (PLAYERS, 2, D, B), ((0, 128), (2, 2)), -0.2, 0.2)), 30.0, 3000.0)
    counts = draw_counts(jax.random.fold_in(keys[3], 71), 0)
    return {"factors": factors, "state": state, "counts": counts}


clip_bound = 2.0

def residual_of(scores, count_tile):
    amount = count_tile.astype(jnp.float32)
    present = count_tile > 0
    clamped = jnp.maximum(amount, 1.0)
    weight = 0.1 + 0.25 * jnp.sqrt(clamped)
    kept = weight * jnp.clip(scores - jnp.log(clamped), -clip_bound, clip_bound)
    return jnp.where(present, kept, 0.5 * jax.nn.sigmoid(scores))

def meeting(operands):
    upper_block, lower_block, count_tile = operands
    scores = jnp.dot(upper_block.T, lower_block, precision=lax.Precision.HIGHEST, preferred_element_type=jnp.float32)
    residual = residual_of(scores, count_tile)
    grad_upper = jnp.dot(lower_block, residual.T, precision=lax.Precision.HIGHEST, preferred_element_type=jnp.float32)
    grad_lower = jnp.dot(upper_block, residual, precision=lax.Precision.HIGHEST, preferred_element_type=jnp.float32)
    return (grad_upper, grad_lower)

def rotate(upper, lower):
    players = upper.shape[0]
    new_upper = jnp.concatenate([upper[:1], lower[:1], upper[1:players - 1]], axis=0)
    new_lower = jnp.concatenate([lower[1:], upper[players - 1:]], axis=0)
    return (new_upper, new_lower)

def rotate_back(upper, lower):
    players = upper.shape[0]
    old_upper = jnp.concatenate([upper[:1], upper[2:], lower[players - 1:]], axis=0)
    old_lower = jnp.concatenate([upper[1:2], lower[:players - 1]], axis=0)
    return (old_upper, old_lower)

def reference(factors, state, counts):
    upper = factors[:, 0]
    lower = factors[:, 1]
    acc_upper = jnp.zeros_like(upper)
    acc_lower = jnp.zeros_like(lower)
    for turn in range(ROUNDS):
        grad_upper, grad_lower = lax.map(meeting, (upper, lower, counts[:, turn]))
        acc_upper = acc_upper + grad_upper
        acc_lower = acc_lower + grad_lower
        if turn < ROUNDS - 1:
            upper, lower = rotate(upper, lower)
            acc_upper, acc_lower = rotate(acc_upper, acc_lower)
    for turn in range(ROUNDS - 1):
        acc_upper, acc_lower = rotate_back(acc_upper, acc_lower)
    grad = jnp.stack([acc_upper, acc_lower], axis=1)
    new_state = state + grad * grad
    step = grad / jnp.sqrt(new_state)
    return (step, new_state)
```

```python
import functools

import jax
import jax.numpy as jnp
from jax import lax
from jax.experimental import pallas as pl
from jax.experimental.pallas import tpu as pltpu
from jax.sharding import PartitionSpec as P

MESH = pl.DeviceIdType.MESH
BF16 = jnp.bfloat16
F32 = jnp.float32
clip_bound = 2.0

A_AT, B_AT, FIXED, SLOTS = 0, 4, 9, 10


def residual_of(scores, count_tile):
    amount = count_tile.astype(F32)
    present = count_tile > 0
    clamped = jnp.maximum(amount, 1.0)
    weight = 0.1 + 0.25 * jnp.sqrt(clamped)
    kept = weight * jnp.clip(scores - jnp.log(clamped), -clip_bound, clip_bound)
    return jnp.where(present, kept, 0.5 * jax.nn.sigmoid(scores))


def split(value):
    high = value.astype(BF16)
    return high, (value - high.astype(F32)).astype(BF16)


def dot3(left, right, dims):
    (lh, ll), (rh, rl) = left, right

    def one(a, b):
        return lax.dot_general(a, b, (dims, ((), ())), preferred_element_type=F32)

    return one(lh, rh) + one(lh, rl) + one(ll, rh)


def kernel(
    chips, tile, factors, counts, out,
    x, g, from_core, from_chain, swapped, extra, tiles, uh, ul, lh, ll,
    load_sem, count_sem,
    in_send, in_recv, fix_send, fix_recv,
    chain_send, chain_recv, core_send, core_recv,
    gcore_send, gcore_recv, gchain_send, gchain_recv,
    out_send, out_recv, gfix_send, gfix_recv,
):
    p, q = lax.axis_index("blk"), lax.axis_index("rep")
    c, h = p // 2, p % 2
    differs = (h + q) % 2
    same = differs == 0
    other = differs == 1
    first = c == 0
    sibling = (c * 2 + 1 - h, q)
    partner = (c * 2 + 1 - h, 1 - q)
    at_end = c == chips - 1
    right = (jnp.where(at_end, c, c + 1) * 2 + h, jnp.where(at_end, 1 - q, q))
    left = (jnp.maximum(c - 1, 0) * 2 + h, q)
    even = q == 0

    def pick(a, b):
        return tuple(jnp.where(even, i, j) for i, j in zip(a, b))

    down_a, up_a = pick(right, left), pick(left, right)
    down_b, up_b = up_a, down_a
    has_up_a = jnp.logical_or(q == 1, c > 0)
    has_down_a = jnp.logical_or(q == 0, c > 0)
    has_up_b, has_down_b = has_down_a, has_up_a
    alias_a = jnp.logical_and(first, q == 0)
    alias_b = jnp.logical_and(first, q == 1)
    is_fixed = p == 0
    fixed_peer = (p, 1 - q)

    def slot_a(k):
        return jnp.where(alias_a, B_AT + k, A_AT + k)

    def slot_b(k):
        return jnp.where(jnp.logical_and(alias_b, k >= 1), A_AT + k - 1, B_AT + k)

    def remote(src, dst, send, recv, to):
        return pltpu.make_async_remote_copy(
            src_ref=src, dst_ref=dst, send_sem=send, recv_sem=recv, device_id=to, device_id_type=MESH
        )

    def load(i):
        at = jnp.where(i == 0, A_AT, B_AT)
        which = jnp.where(i == 0, q, 1 - q)
        return pltpu.make_async_copy(factors.at[which], x.at[at, h], load_sem.at[i])

    def swap_in(i):
        at = jnp.where(i == 0, A_AT, B_AT)
        which = jnp.where(i == 0, 1 - q, q)
        return remote(factors.at[which], x.at[at, 1 - h], in_send.at[i], in_recv.at[i], partner)

    def swap_in_arrival(i):
        at = jnp.where(i == 0, A_AT, B_AT)
        return remote(factors.at[0], x.at[at, h], in_send.at[i], in_recv.at[i], partner)

    def counts_in(k):
        return pltpu.make_async_copy(counts.at[2 * k + differs], tiles.at[k], count_sem.at[k])

    def chain_a(k):
        return remote(x.at[slot_a(k), h], x.at[A_AT + k + 1, h], chain_send.at[A_AT + k], chain_recv.at[A_AT + k + 1], down_a)

    def chain_a_arrival(k):
        return remote(x.at[0, h], x.at[A_AT + k, h], chain_send.at[A_AT + k], chain_recv.at[A_AT + k], up_a)

    def chain_b(k):
        return remote(x.at[slot_b(k), h], x.at[B_AT + k + 1, h], chain_send.at[B_AT + k], chain_recv.at[B_AT + k + 1], down_b)

    def chain_b_arrival(k):
        return remote(x.at[0, h], x.at[B_AT + k, h], chain_send.at[B_AT + k], chain_recv.at[B_AT + k], up_b)

    def to_core(at):
        return remote(x.at[at, h], x.at[at, h], core_send.at[at], core_recv.at[at], sibling)

    def from_core_arrival(at):
        return remote(x.at[at, 1 - h], x.at[at, 1 - h], core_send.at[at], core_recv.at[at], sibling)

    def g_core(at):
        return remote(g.at[at, 1 - h], from_core.at[at], gcore_send.at[at], gcore_recv.at[at], sibling)

    def g_chain(at, to):
        return remote(g.at[at, h], from_chain.at[at - 1], gchain_send.at[at], gchain_recv.at[at - 1], to)

    def g_chain_arrival(at, to):
        return remote(g.at[at, h], from_chain.at[at], gchain_send.at[at], gchain_recv.at[at], to)

    def swap_out(i):
        at = jnp.where(i == 0, A_AT, B_AT)
        return remote(g.at[at, h], swapped.at[i], out_send.at[i], out_recv.at[i], partner)

    fixed_in = remote(factors.at[0], x.at[FIXED, 0], fix_send, fix_recv, fixed_peer)
    fixed_own = pltpu.make_async_copy(factors.at[0], x.at[FIXED, 1], load_sem.at[2])
    fixed_out = remote(g.at[FIXED, 1 - q], extra, gfix_send, gfix_recv, fixed_peer)
    fixed_giver = jnp.logical_and(is_fixed, q == 0)
    fixed_taker = jnp.logical_and(is_fixed, q == 1)

    @pl.when(same)
    def _():
        load(0).start()
        load(1).start()

    @pl.when(fixed_taker)
    def _():
        fixed_own.start()

    for k in range(4):
        counts_in(k).start()

    barrier = pltpu.get_barrier_semaphore()

    def greet(to):
        pl.semaphore_signal(barrier, inc=1, device_id=to, device_id_type=MESH)

    greet(sibling)
    greet(right)

    @pl.when(c > 0)
    def _():
        greet(left)

    @pl.when(other)
    def _():
        greet(partner)

    @pl.when(is_fixed)
    def _():
        greet(fixed_peer)

    greeted = 2 + jnp.where(c > 0, 1, 0) + differs + jnp.where(is_fixed, 1, 0)
    pl.semaphore_wait(barrier, greeted)

    @pl.when(other)
    def _():
        swap_in(0).start()
        swap_in(1).start()

    @pl.when(fixed_giver)
    def _():
        fixed_in.start()

    @pl.loop(0, SLOTS)
    def _(at):
        g[at] = jnp.zeros_like(g[at])

    @pl.when(fixed_taker)
    def _():
        fixed_own.wait()
        fixed_in.wait_recv()

    def relay_b(s):
        @pl.when(jnp.logical_and(has_down_b, s < 4))
        def _():
            chain_b(s).start()

        @pl.when(jnp.logical_or(has_up_b, s == 0))
        def _():
            to_core(B_AT + s).start()

    def relay_a(s):
        @pl.when(jnp.logical_and(has_down_a, s < 3))
        def _():
            chain_a(s).start()

        @pl.when(jnp.logical_or(has_up_a, s == 0))
        def _():
            to_core(A_AT + s).start()

    def meeting(k):
        a, b = slot_a(k), slot_b(k + differs)
        upper = jnp.where(is_fixed, jnp.where(even, A_AT, FIXED), jnp.where(even, a, b))
        lower = jnp.where(even, b, a)
        g_upper = jnp.where(is_fixed, FIXED, upper)
        counts_in(k).wait()
        for half in range(2):
            uh[half], ul[half] = split(x[upper, half])
            lh[half], ll[half] = split(x[lower, half])
        items = x.shape[-1]

        for start in range(0, items, tile):
            rows = pl.ds(start, tile)
            scores = 0.0
            for half in range(2):
                scores += dot3((uh[half, :, rows], ul[half, :, rows]), (lh[half], ll[half]), ((0,), (0,)))
            r = split(residual_of(scores, tiles[k, rows, :]))
            for half in range(2):
                g[lower, half] += dot3((uh[half, :, rows], ul[half, :, rows]), r, ((1,), (0,)))
                g[g_upper, half, :, rows] += dot3((lh[half], ll[half]), r, ((1,), (1,)))

    @pl.loop(0, 5)
    def _(s):
        @pl.when(s == 0)
        def _():
            @pl.when(same)
            def _():
                load(1).wait()

            @pl.when(other)
            def _():
                swap_in_arrival(1).wait_recv()

        @pl.when(jnp.logical_and(s > 0, has_up_b))
        def _():
            chain_b_arrival(s).wait_recv()

        relay_b(s)

        @pl.when(s == 0)
        def _():
            @pl.when(same)
            def _():
                load(0).wait()

            @pl.when(other)
            def _():
                swap_in_arrival(0).wait_recv()

        @pl.when(jnp.logical_and(jnp.logical_and(s > 0, s < 4), has_up_a))
        def _():
            chain_a_arrival(s).wait_recv()

        @pl.when(s < 4)
        def _():
            relay_a(s)

        @pl.when(jnp.logical_and(s == 1, other))
        def _():
            from_core_arrival(B_AT).wait_recv()

        @pl.when(s > 0)
        def _():
            k = s - 1

            @pl.when(jnp.logical_or(has_up_a, k == 0))
            def _():
                from_core_arrival(A_AT + k).wait_recv()

            @pl.when(jnp.logical_or(has_up_b, k + differs == 0))
            def _():
                from_core_arrival(B_AT + k + differs).wait_recv()

            meeting(k)

            @pl.when(s > 1)
            def _():
                g_core(A_AT + k - 1).start()
                g_core(B_AT + k - 1).start()

    @pl.when(jnp.logical_and(same, has_up_b))
    def _():
        from_core_arrival(B_AT + 4).wait_recv()

    g_core(B_AT + 4).start()
    g_core(A_AT + 3).start()
    g_core(B_AT + 3).start()

    @pl.when(is_fixed)
    def _():
        fixed_out.start()

    def send_back(at, alias, k, last, has_down, has_up, down, up):
        g_core(at).wait_recv()
        g[at, h] += from_core[at]

        @pl.when(jnp.logical_and(k < last, has_down))
        def _():
            g_chain_arrival(at, down).wait_recv()
            g[alias, h] += from_chain[at]

        @pl.when(jnp.logical_and(k > 0, has_up))
        def _():
            g_chain(at, up).start()

    @pl.loop(0, 5)
    def _(step):
        k = 4 - step

        @pl.when(k < 4)
        def _():
            send_back(A_AT + k, slot_a(k), k, 3, has_down_a, has_up_a, down_a, up_a)

        send_back(B_AT + k, slot_b(k), k, 4, has_down_b, has_up_b, down_b, up_b)

    @pl.when(other)
    def _():
        swap_out(0).start()
        swap_out(1).start()

    @pl.when(same)
    def _():
        out[q] = g[A_AT, h]
        out[1 - q] = g[B_AT, h]

    @pl.when(other)
    def _():
        swap_out(0).wait_recv()
        out[1 - q] = swapped[0]
        swap_out(1).wait_recv()
        out[q] = swapped[1]

    @pl.when(is_fixed)
    def _():
        fixed_out.wait_recv()
        out[0] += g[FIXED, q] + extra[...]

    @pl.when(other)
    def _():
        for i in range(2):
            swap_in(i).wait_send()
            swap_out(i).wait_send()

    @pl.when(fixed_giver)
    def _():
        fixed_in.wait_send()

    @pl.when(is_fixed)
    def _():
        fixed_out.wait_send()

    @pl.loop(0, 5)
    def _(k):
        @pl.when(jnp.logical_or(has_up_b, k == 0))
        def _():
            to_core(B_AT + k).wait_send()

        @pl.when(jnp.logical_and(has_down_b, k < 4))
        def _():
            chain_b(k).wait_send()

        g_core(B_AT + k).wait_send()

        @pl.when(jnp.logical_and(has_up_b, k > 0))
        def _():
            g_chain(B_AT + k, up_b).wait_send()

        @pl.when(k < 4)
        def _():
            @pl.when(jnp.logical_or(has_up_a, k == 0))
            def _():
                to_core(A_AT + k).wait_send()

            @pl.when(jnp.logical_and(has_down_a, k < 3))
            def _():
                chain_a(k).wait_send()

            g_core(A_AT + k).wait_send()

            @pl.when(jnp.logical_and(has_up_a, k > 0))
            def _():
                g_chain(A_AT + k, up_a).wait_send()


def solution(mesh):
    players = mesh.shape["blk"]
    chips = players // 2

    def body(factors, state, counts):
        share, items = factors.shape[2], factors.shape[3]
        tile = min(256, items)
        dma = pltpu.SemaphoreType.DMA
        grad = pl.pallas_call(
            functools.partial(kernel, chips, tile),
            out_shape=jax.ShapeDtypeStruct((2, share, items), F32),
            in_specs=[pl.BlockSpec(memory_space=pl.ANY)] * 2,
            out_specs=pl.BlockSpec(memory_space=pltpu.VMEM),
            scratch_shapes=[
                pltpu.VMEM((SLOTS, 2, share, items), F32),
                pltpu.VMEM((SLOTS, 2, share, items), F32),
                pltpu.VMEM((9, share, items), F32),
                pltpu.VMEM((9, share, items), F32),
                pltpu.VMEM((2, share, items), F32),
                pltpu.VMEM((share, items), F32),
                pltpu.VMEM((4, items, items), jnp.int32),
                pltpu.VMEM((2, share, items), BF16),
                pltpu.VMEM((2, share, items), BF16),
                pltpu.VMEM((2, share, items), BF16),
                pltpu.VMEM((2, share, items), BF16),
                dma((3,)), dma((4,)),
                dma((2,)), dma((2,)), dma, dma,
                dma((9,)), dma((9,)), dma((9,)), dma((9,)),
                dma((9,)), dma((9,)), dma((9,)), dma((9,)),
                dma((2,)), dma((2,)), dma, dma,
            ],
            compiler_params=pltpu.CompilerParams(
                collective_id=0, has_side_effects=True, vmem_limit_bytes=60 * 1024 * 1024
            ),
        )(factors[0], counts[0])
        grad = grad[None]
        new_state = state + grad * grad
        step = grad / jnp.sqrt(new_state)
        return (step, new_state)

    in_specs = (
        P("blk", None, "rep", None),
        P("blk", None, "rep", None),
        P("blk", None, None, None),
    )
    out_specs = (P("blk", None, "rep", None), P("blk", None, "rep", None))
    return jax.shard_map(body, mesh=mesh, in_specs=in_specs, out_specs=out_specs, check_vma=False)
```

```python
import functools

import jax
import jax.numpy as jnp
from jax import lax
from jax.experimental import pallas as pl
from jax.experimental.pallas import tpu as pltpu
from jax.sharding import PartitionSpec as P

MESH = pl.DeviceIdType.MESH
BF16 = jnp.bfloat16
F32 = jnp.float32
clip_bound = 2.0

A_AT, B_AT, FIXED, SLOTS = 0, 4, 9, 10


def residual_of(scores, count_tile):
    amount = count_tile.astype(F32)
    present = count_tile > 0
    clamped = jnp.maximum(amount, 1.0)
    weight = 0.1 + 0.25 * jnp.sqrt(clamped)
    kept = weight * jnp.clip(scores - jnp.log(clamped), -clip_bound, clip_bound)
    return jnp.where(present, kept, 0.5 * jax.nn.sigmoid(scores))


def split(value):
    high = value.astype(BF16)
    return high, (value - high.astype(F32)).astype(BF16)


def dot3(left, right, dims):
    (lh, ll), (rh, rl) = left, right

    def one(a, b):
        return lax.dot_general(a, b, (dims, ((), ())), preferred_element_type=F32)

    return one(lh, rh) + one(lh, rl) + one(ll, rh)


def kernel(
    chips, tile, factors, counts, out,
    x, g, from_core, from_chain, returned, swapped, extra, tiles, uh, ul, lh, ll,
    load_sem, count_sem,
    in_send, in_recv, fix_send, fix_recv,
    out_block_send, block_recv, core_send, core_recv,
    gcore_send, gcore_recv, gback_send, gchain_recv, returned_recv,
    out_send, out_recv, gfix_send, gfix_recv,
):
    p, q = lax.axis_index("blk"), lax.axis_index("rep")
    c, h = p // 2, p % 2
    differs = (h + q) % 2
    same = differs == 0
    other = differs == 1
    even, odd = q == 0, q == 1

    def both(*conditions):
        return functools.reduce(jnp.logical_and, conditions)

    def either(*conditions):
        return functools.reduce(jnp.logical_or, conditions)

    def pick(condition, a, b):
        return tuple(jnp.where(condition, i, j) for i, j in zip(a, b))

    def ahead(n):
        over = c + n >= chips
        return (jnp.where(over, 2 * chips - 1 - c - n, c + n) * 2 + h, jnp.where(over, 1 - q, q))

    def at_chip(chip):
        return (jnp.maximum(chip, 0) * 2 + h, q)

    sibling = (c * 2 + 1 - h, q)
    partner = (c * 2 + 1 - h, 1 - q)
    fixed_peer = (p, 1 - q)
    right, left = ahead(1), at_chip(c - 1)
    down_a, up_a = pick(even, right, left), pick(even, left, right)
    down_b, up_b = up_a, down_a
    has_up_a = either(odd, c > 0)
    has_down_a = either(even, c > 0)
    has_up_b, has_down_b = has_down_a, has_up_a
    alias_a, alias_b = both(even, c == 0), both(odd, c == 0)
    is_fixed = p == 0

    has_b3, has_b4 = either(even, c >= 2), either(even, c >= 1)
    far = (
        (either(even, c >= 3, c == 0), pick(even, ahead(3), at_chip(jnp.where(c == 0, 2, c - 3))),
         jnp.where(alias_a, B_AT, A_AT), jnp.where(alias_b, B_AT + 3, A_AT + 3)),
        (either(odd, c >= 1), pick(odd, ahead(3), at_chip(jnp.where(c >= 3, c - 3, 3 - c))),
         B_AT, jnp.where(both(even, c < 3), A_AT + 3, B_AT + 3)),
        (either(odd, c >= 4), pick(odd, ahead(4), at_chip(c - 4)), B_AT, B_AT + 4),
        (both(odd, c <= 2), at_chip(3 - c), A_AT, B_AT + 4),
    )
    from_a3 = (has_up_a, pick(even, at_chip(jnp.where(c >= 3, c - 3, 3 - c)), ahead(3)),
               jnp.where(both(even, c < 3), 1, 0))
    from_b3 = (has_b3, pick(even, ahead(3), at_chip(jnp.where(c >= 3, c - 3, 2 - c))),
               jnp.where(both(odd, c == 2), 0, 1))
    from_b4 = (has_b4, pick(even, ahead(4), at_chip(jnp.where(c >= 4, c - 4, 3 - c))),
               jnp.where(both(odd, c < 4), 3, 2))

    def slot_a(k):
        return jnp.where(alias_a, B_AT + k, A_AT + k)

    def slot_b(k):
        at = jnp.where(both(alias_b, k >= 1), A_AT + k - 1, B_AT + k)
        return jnp.where(both(odd, c == 1, k == 3), A_AT, at)

    def remote(src, dst, send, recv, to):
        return pltpu.make_async_remote_copy(
            src_ref=src, dst_ref=dst, send_sem=send, recv_sem=recv, device_id=to, device_id_type=MESH
        )

    def load(i):
        at = jnp.where(i == 0, A_AT, B_AT)
        which = jnp.where(i == 0, q, 1 - q)
        return pltpu.make_async_copy(factors.at[which], x.at[at, h], load_sem.at[i])

    def swap_in(i):
        at = jnp.where(i == 0, A_AT, B_AT)
        which = jnp.where(i == 0, 1 - q, q)
        return remote(factors.at[which], x.at[at, 1 - h], in_send.at[i], in_recv.at[i], partner)

    def swap_in_arrival(i):
        at = jnp.where(i == 0, A_AT, B_AT)
        return remote(factors.at[0], x.at[at, h], in_send.at[i], in_recv.at[i], partner)

    def counts_in(k):
        return pltpu.make_async_copy(counts.at[2 * k + differs], tiles.at[k], count_sem.at[k])

    def chain_a(k):
        to = A_AT + k + 1
        return remote(x.at[slot_a(k), h], x.at[to, h], out_block_send.at[4 + k], block_recv.at[to], down_a)

    def chain_b(k):
        to = B_AT + k + 1
        return remote(x.at[slot_b(k), h], x.at[to, h], out_block_send.at[6 + k], block_recv.at[to], down_b)

    def far_block(i):
        _, to, at, into = far[i]
        return remote(x.at[at, h], x.at[into, h], out_block_send.at[i], block_recv.at[into], to)

    def arrival(at):
        return remote(x.at[at, h], x.at[at, h], out_block_send.at[0], block_recv.at[at], sibling)

    def to_core(at):
        return remote(x.at[at, h], x.at[at, h], core_send.at[at], core_recv.at[at], sibling)

    def from_core_arrival(at):
        return remote(x.at[at, 1 - h], x.at[at, 1 - h], core_send.at[at], core_recv.at[at], sibling)

    def g_core(at):
        return remote(g.at[at, 1 - h], from_core.at[at], gcore_send.at[at], gcore_recv.at[at], sibling)

    def g_chain(at, to):
        return remote(g.at[at, h], from_chain.at[at - 1], gback_send.at[at], gchain_recv.at[at - 1], to)

    def g_chain_arrival(at):
        return remote(g.at[at, h], from_chain.at[at], gback_send.at[at], gchain_recv.at[at], sibling)

    def g_return(at, source):
        _, to, i = source
        return remote(g.at[at, h], returned.at[i], gback_send.at[at], returned_recv.at[i], to)

    def g_return_arrival(i):
        return remote(g.at[0, h], returned.at[i], gback_send.at[0], returned_recv.at[i], sibling)

    def swap_out(i):
        at = jnp.where(i == 0, A_AT, B_AT)
        return remote(g.at[at, h], swapped.at[i], out_send.at[i], out_recv.at[i], partner)

    fixed_in = remote(factors.at[0], x.at[FIXED, 0], fix_send, fix_recv, fixed_peer)
    fixed_own = pltpu.make_async_copy(factors.at[0], x.at[FIXED, 1], load_sem.at[2])
    fixed_out = remote(g.at[FIXED, 1 - q], extra, gfix_send, gfix_recv, fixed_peer)
    fixed_giver = both(is_fixed, even)
    fixed_taker = both(is_fixed, odd)

    def when(condition, action):
        @pl.when(condition)
        def _():
            action()

    @pl.when(same)
    def _():
        load(0).start()
        load(1).start()

    when(fixed_taker, fixed_own.start)
    for k in range(4):
        counts_in(k).start()

    barrier = pltpu.get_barrier_semaphore()
    peers = [
        (None, sibling), (None, right), (c > 0, left), (other, partner), (is_fixed, fixed_peer),
        *[(f[0], f[1]) for f in far], from_a3[:2], from_b3[:2], from_b4[:2],
    ]
    greeted = 0
    for condition, to in peers:
        def greet(to=to):
            pl.semaphore_signal(barrier, inc=1, device_id=to, device_id_type=MESH)

        if condition is None:
            greet()
            greeted += 1
        else:
            when(condition, greet)
            greeted += jnp.where(condition, 1, 0)
    pl.semaphore_wait(barrier, greeted)

    @pl.when(other)
    def _():
        swap_in(1).start()
        swap_in(0).start()

    when(fixed_giver, fixed_in.start)

    @pl.loop(0, SLOTS)
    def _(at):
        g[at] = jnp.zeros_like(g[at])

    for i, stream, has_down in ((1, chain_b, has_down_b), (0, chain_a, has_down_a)):
        when(same, load(i).wait)
        when(other, swap_in_arrival(i).wait_recv)
        when(has_down, stream(0).start)
        to_core(A_AT if i == 0 else B_AT).start()
    for i in (1, 0, 2, 3):
        when(far[i][0], far_block(i).start)

    @pl.when(fixed_taker)
    def _():
        fixed_own.wait()
        fixed_in.wait_recv()

    def meeting(k):
        a, b = slot_a(k), slot_b(k + differs)
        upper = jnp.where(is_fixed, jnp.where(even, A_AT, FIXED), jnp.where(even, a, b))
        lower = jnp.where(even, b, a)
        g_upper = jnp.where(is_fixed, FIXED, upper)
        counts_in(k).wait()
        for half in range(2):
            uh[half], ul[half] = split(x[upper, half])
            lh[half], ll[half] = split(x[lower, half])
        items = x.shape[-1]

        for start in range(0, items, tile):
            rows = pl.ds(start, tile)
            scores = 0.0
            for half in range(2):
                scores += dot3((uh[half, :, rows], ul[half, :, rows]), (lh[half], ll[half]), ((0,), (0,)))
            r = split(residual_of(scores, tiles[k, rows, :]))
            for half in range(2):
                g[lower, half] += dot3((uh[half, :, rows], ul[half, :, rows]), r, ((1,), (0,)))
                g[g_upper, half, :, rows] += dot3((lh[half], ll[half]), r, ((1,), (1,)))

    has = {1: has_up_a, 2: has_up_a, 3: has_up_a, 5: has_up_b, 6: has_up_b, 7: has_b3, 8: has_b4}

    def pass_on(at, stream=None, has_down=None):
        when(has[at], arrival(at).wait_recv)
        if stream is not None:
            when(has_down, stream(1).start)
        when(has[at], to_core(at).start)

    def other_half(at, condition=None):
        conditions = [i for i in (has.get(at), condition) if i is not None]
        if conditions:
            when(both(*conditions), from_core_arrival(at).wait_recv)
        else:
            from_core_arrival(at).wait_recv()

    def gathered(at):
        g_core(at).wait_recv()
        g[at, h] += from_core[at]

    def give_back(at, source):
        gathered(at)
        when(source[0], g_return(at, source).start)

    order = (0, jnp.where(same, 1, 3), jnp.where(same, 3, 2), jnp.where(same, 2, 1))

    @pl.loop(0, 4)
    def _(turn):
        @pl.when(turn == 0)
        def _():
            pass_on(B_AT + 1, chain_b, has_down_b)
            pass_on(A_AT + 1, chain_a, has_down_a)
            other_half(B_AT)
            other_half(A_AT)
            other_half(B_AT + 1, other)

        @pl.when(turn == 1)
        def _():
            pass_on(B_AT + 4)
            pass_on(B_AT + 3)
            pass_on(A_AT + 3)
            other_half(A_AT + 1, same)
            other_half(B_AT + 1, same)
            other_half(A_AT + 3, other)
            other_half(B_AT + 3, other)
            other_half(B_AT + 4, other)

        @pl.when(turn == 2)
        def _():
            g_core(B_AT + 4).start()
            pass_on(B_AT + 2)
            pass_on(A_AT + 2)
            other_half(A_AT + 3, same)
            other_half(B_AT + 3, same)
            other_half(A_AT + 2, either(other, alias_b))
            other_half(B_AT + 2, other)

        @pl.when(turn == 3)
        def _():
            g_core(A_AT + 3).start()
            g_core(B_AT + 3).start()
            give_back(B_AT + 4, from_b4)
            give_back(A_AT + 3, from_a3)
            give_back(B_AT + 3, from_b3)
            other_half(A_AT + 1, other)
            other_half(A_AT + 2, both(same, jnp.logical_not(alias_b)))
            other_half(B_AT + 2, same)

        k = jnp.where(turn == 0, order[0], jnp.where(turn == 1, order[1], jnp.where(turn == 2, order[2], order[3])))
        meeting(k)

    for k in (2, 1, 0):
        g_core(A_AT + k).start()
        g_core(B_AT + k).start()
    when(is_fixed, fixed_out.start)

    def chained(at, alias, has_down):
        @pl.when(has_down)
        def _():
            g_chain_arrival(at).wait_recv()
            g[alias, h] += from_chain[at]

    def add_returned(i, at):
        @pl.when(far[i][0])
        def _():
            g_return_arrival(i).wait_recv()
            g[at, h] += returned[i]

    gathered(A_AT + 2)
    when(has_up_a, g_chain(A_AT + 2, up_a).start)
    gathered(B_AT + 2)
    when(has_up_b, g_chain(B_AT + 2, up_b).start)
    gathered(A_AT + 1)
    gathered(B_AT + 1)
    chained(A_AT + 1, slot_a(1), has_down_a)
    when(has_up_a, g_chain(A_AT + 1, up_a).start)
    chained(B_AT + 1, slot_b(1), has_down_b)
    when(has_up_b, g_chain(B_AT + 1, up_b).start)
    gathered(A_AT)
    gathered(B_AT)
    for i in (0, 1, 2, 3):
        add_returned(i, far[i][2])
    chained(A_AT, slot_a(0), has_down_a)

    @pl.when(other)
    def _():
        swap_out(0).start()

    @pl.when(same)
    def _():
        out[q] = g[A_AT, h]

    chained(B_AT, B_AT, has_down_b)

    @pl.when(other)
    def _():
        swap_out(1).start()
        swap_out(0).wait_recv()
        out[1 - q] = swapped[0]
        swap_out(1).wait_recv()
        out[q] = swapped[1]

    @pl.when(same)
    def _():
        out[1 - q] = g[B_AT, h]

    @pl.when(is_fixed)
    def _():
        fixed_out.wait_recv()
        out[0] += g[FIXED, q] + extra[...]

    other_half(B_AT + 4, same)

    @pl.when(other)
    def _():
        for i in range(2):
            swap_in(i).wait_send()
            swap_out(i).wait_send()

    when(fixed_giver, fixed_in.wait_send)
    when(is_fixed, fixed_out.wait_send)
    for i in range(4):
        when(far[i][0], far_block(i).wait_send)
    for k in range(2):
        when(has_down_a, chain_a(k).wait_send)
        when(has_down_b, chain_b(k).wait_send)
    for at in range(9):
        if at in has:
            when(has[at], to_core(at).wait_send)
        else:
            to_core(at).wait_send()
        g_core(at).wait_send()
    for k in (1, 2):
        when(has_up_a, g_chain(A_AT + k, up_a).wait_send)
        when(has_up_b, g_chain(B_AT + k, up_b).wait_send)
    when(from_a3[0], g_return(A_AT + 3, from_a3).wait_send)
    when(from_b3[0], g_return(B_AT + 3, from_b3).wait_send)
    when(from_b4[0], g_return(B_AT + 4, from_b4).wait_send)


def solution(mesh):
    players = mesh.shape["blk"]
    chips = players // 2

    def body(factors, state, counts):
        share, items = factors.shape[2], factors.shape[3]
        tile = min(512, items)
        dma = pltpu.SemaphoreType.DMA
        grad = pl.pallas_call(
            functools.partial(kernel, chips, tile),
            out_shape=jax.ShapeDtypeStruct((2, share, items), F32),
            in_specs=[pl.BlockSpec(memory_space=pl.ANY)] * 2,
            out_specs=pl.BlockSpec(memory_space=pltpu.VMEM),
            scratch_shapes=[
                pltpu.VMEM((SLOTS, 2, share, items), F32),
                pltpu.VMEM((SLOTS, 2, share, items), F32),
                pltpu.VMEM((9, share, items), F32),
                pltpu.VMEM((6, share, items), F32),
                pltpu.VMEM((4, share, items), F32),
                pltpu.VMEM((2, share, items), F32),
                pltpu.VMEM((share, items), F32),
                pltpu.VMEM((4, items, items), jnp.int32),
                pltpu.VMEM((2, share, items), BF16),
                pltpu.VMEM((2, share, items), BF16),
                pltpu.VMEM((2, share, items), BF16),
                pltpu.VMEM((2, share, items), BF16),
                dma((3,)), dma((4,)),
                dma((2,)), dma((2,)), dma, dma,
                dma((8,)), dma((9,)), dma((9,)), dma((9,)),
                dma((9,)), dma((9,)), dma((9,)), dma((6,)), dma((4,)),
                dma((2,)), dma((2,)), dma, dma,
            ],
            compiler_params=pltpu.CompilerParams(
                collective_id=0, has_side_effects=True, vmem_limit_bytes=60 * 1024 * 1024
            ),
        )(factors[0], counts[0])
        grad = grad[None]
        new_state = state + grad * grad
        step = grad / jnp.sqrt(new_state)
        return (step, new_state)

    in_specs = (
        P("blk", None, "rep", None),
        P("blk", None, "rep", None),
        P("blk", None, None, None),
    )
    out_specs = (P("blk", None, "rep", None), P("blk", None, "rep", None))
    return jax.shard_map(body, mesh=mesh, in_specs=in_specs, out_specs=out_specs, check_vma=False)
```

```python
import functools

import jax
import jax.numpy as jnp
from jax import lax
from jax.experimental import pallas as pl
from jax.experimental.pallas import tpu as pltpu
from jax.sharding import PartitionSpec as P

MESH = pl.DeviceIdType.MESH
BF16 = jnp.bfloat16
F32 = jnp.float32
clip_bound = 2.0

A_AT, B_AT, FIXED, SLOTS = 0, 4, 9, 10
LANES = 128


def residual_of(scores, count_tile):
    amount = count_tile.astype(F32)
    present = count_tile > 0
    clamped = jnp.maximum(amount, 1.0)
    weight = 0.1 + 0.25 * jnp.sqrt(clamped)
    kept = weight * jnp.clip(scores - jnp.log(clamped), -clip_bound, clip_bound)
    return jnp.where(present, kept, 0.5 * jax.nn.sigmoid(scores))


def split(value):
    high = value.astype(BF16)
    return high, (value - high.astype(F32)).astype(BF16)


def dot3(left, right, dims):
    (lh, ll), (rh, rl) = left, right

    def one(a, b):
        return lax.dot_general(a, b, (dims, ((), ())), preferred_element_type=F32)

    return one(lh, rh) + one(lh, rl) + one(ll, rh)


def pack(blocks):
    two, share, items = blocks.shape
    return blocks.reshape(two, share, items // LANES, LANES).transpose(1, 2, 0, 3).reshape(-1, LANES)


def unpack(rows, dims):
    one, two, share, items = dims
    return rows.reshape(share, items // LANES, two, LANES).transpose(2, 0, 1, 3).reshape(dims)


def kernel(
    chips, tile, factors, counts, out,
    x, g, raw, mine, from_core, from_chain, returned, swapped, extra, tiles, uh, ul, lh, ll,
    load_sem, count_sem,
    in_send, in_recv, fix_send, fix_recv,
    out_block_send, block_recv, core_send, core_recv,
    gcore_send, gcore_recv, gback_send, gchain_recv, returned_recv,
    out_send, out_recv, gfix_send, gfix_recv,
):
    p, q = lax.axis_index("blk"), lax.axis_index("rep")
    c, h = p // 2, p % 2
    differs = (h + q) % 2
    same = differs == 0
    other = differs == 1
    even, odd = q == 0, q == 1

    def both(*conditions):
        return functools.reduce(jnp.logical_and, conditions)

    def either(*conditions):
        return functools.reduce(jnp.logical_or, conditions)

    def pick(condition, a, b):
        return tuple(jnp.where(condition, i, j) for i, j in zip(a, b))

    def ahead(n):
        over = c + n >= chips
        return (jnp.where(over, 2 * chips - 1 - c - n, c + n) * 2 + h, jnp.where(over, 1 - q, q))

    def at_chip(chip):
        return (jnp.maximum(chip, 0) * 2 + h, q)

    sibling = (c * 2 + 1 - h, q)
    partner = (c * 2 + 1 - h, 1 - q)
    fixed_peer = (p, 1 - q)
    right, left = ahead(1), at_chip(c - 1)
    down_a, up_a = pick(even, right, left), pick(even, left, right)
    down_b, up_b = up_a, down_a
    has_up_a = either(odd, c > 0)
    has_down_a = either(even, c > 0)
    has_up_b, has_down_b = has_down_a, has_up_a
    alias_a, alias_b = both(even, c == 0), both(odd, c == 0)
    is_fixed = p == 0

    half_way = chips // 2

    def right_fed(chip):
        return both(chip >= half_way, chip < half_way + 3)

    def left_fed(chip):
        return either(both(chip >= half_way - 3, chip < half_way), chip >= chips - 3)

    def fed_a3(to):
        return jnp.where(to[1] == 0, right_fed(to[0] // 2), left_fed(to[0] // 2))

    def fed_b3(to):
        return jnp.where(to[1] == 0, left_fed(to[0] // 2), right_fed(to[0] // 2))

    def fed_b4(to):
        return both(to[1] == 0, to[0] // 2 == chips - 4)

    here = (p, q)
    near = either(both(c >= half_way - 3, c < half_way + 3), c >= chips - 4)
    plain = jnp.logical_not(near)
    send_a2, send_b2 = both(has_down_a, fed_a3(down_a)), both(has_down_b, fed_b3(down_b))
    send_b3 = both(has_down_b, fed_b4(down_b))

    has_b3, has_b4 = either(even, c >= 2), either(even, c >= 1)
    far_to = (
        pick(even, ahead(3), at_chip(jnp.where(c == 0, 2, c - 3))),
        pick(odd, ahead(3), at_chip(jnp.where(c >= 3, c - 3, 3 - c))),
        pick(odd, ahead(4), at_chip(c - 4)),
        at_chip(3 - c),
    )
    first_to_b, second_to_a = alias_b, both(even, c < 3)
    not_fed = (
        jnp.logical_not(jnp.where(first_to_b, fed_b3(far_to[0]), fed_a3(far_to[0]))),
        jnp.logical_not(jnp.where(second_to_a, fed_a3(far_to[1]), fed_b3(far_to[1]))),
        jnp.logical_not(fed_b4(far_to[2])),
    )
    far = (
        (both(either(even, c >= 3, c == 0), not_fed[0]), far_to[0],
         jnp.where(alias_a, B_AT, A_AT), jnp.where(first_to_b, B_AT + 3, A_AT + 3)),
        (both(either(odd, c >= 1), not_fed[1]), far_to[1],
         B_AT, jnp.where(second_to_a, A_AT + 3, B_AT + 3)),
        (both(either(odd, c >= 4), not_fed[2]), far_to[2], B_AT, B_AT + 4),
        (both(odd, c <= 2), far_to[3], A_AT, B_AT + 4),
    )
    from_a3 = (both(has_up_a, jnp.logical_not(fed_a3(here))), pick(even, at_chip(jnp.where(c >= 3, c - 3, 3 - c)), ahead(3)),
               jnp.where(both(even, c < 3), 1, 0))
    from_b3 = (both(has_b3, jnp.logical_not(fed_b3(here))), pick(even, ahead(3), at_chip(jnp.where(c >= 3, c - 3, 2 - c))),
               jnp.where(both(odd, c == 2), 0, 1))
    from_b4 = (both(has_b4, jnp.logical_not(fed_b4(here))), pick(even, ahead(4), at_chip(jnp.where(c >= 4, c - 4, 3 - c))),
               jnp.where(both(odd, c < 4), 3, 2))

    def slot_a(k):
        return jnp.where(alias_a, B_AT + k, A_AT + k)

    def slot_b(k):
        at = jnp.where(both(alias_b, k >= 1), A_AT + k - 1, B_AT + k)
        return jnp.where(both(odd, c == 1, k == 3), A_AT, at)

    def remote(src, dst, send, recv, to):
        return pltpu.make_async_remote_copy(
            src_ref=src, dst_ref=dst, send_sem=send, recv_sem=recv, device_id=to, device_id_type=MESH
        )

    own = pltpu.make_async_copy(factors, mine, load_sem.at[0])
    swap_in = remote(factors, raw, in_send, in_recv, partner)

    def counts_in(k):
        return pltpu.make_async_copy(counts.at[2 * k + differs], tiles.at[k], count_sem.at[k])

    def chain_a(k):
        to = A_AT + k + 1
        return remote(x.at[slot_a(k), h], x.at[to, h], out_block_send.at[4 + k], block_recv.at[to], down_a)

    def chain_b(k):
        to = B_AT + k + 1
        return remote(x.at[slot_b(k), h], x.at[to, h], out_block_send.at[7 + k], block_recv.at[to], down_b)

    def far_block(i):
        _, to, at, into = far[i]
        return remote(x.at[at, h], x.at[into, h], out_block_send.at[i], block_recv.at[into], to)

    def arrival(at):
        return remote(x.at[at, h], x.at[at, h], out_block_send.at[0], block_recv.at[at], sibling)

    def to_core(at):
        return remote(x.at[at, h], x.at[at, h], core_send.at[at], core_recv.at[at], sibling)

    def from_core_arrival(at):
        return remote(x.at[at, 1 - h], x.at[at, 1 - h], core_send.at[at], core_recv.at[at], sibling)

    def g_core(at):
        return remote(g.at[at, 1 - h], from_core.at[at], gcore_send.at[at], gcore_recv.at[at], sibling)

    def g_chain(at, to):
        return remote(g.at[at, h], from_chain.at[at - 1], gback_send.at[at], gchain_recv.at[at - 1], to)

    def g_chain_arrival(at):
        return remote(g.at[at, h], from_chain.at[at], gback_send.at[at], gchain_recv.at[at], sibling)

    def g_return(at, source):
        _, to, i = source
        return remote(g.at[at, h], returned.at[i], gback_send.at[at], returned_recv.at[i], to)

    def g_return_arrival(i):
        return remote(g.at[0, h], returned.at[i], gback_send.at[0], returned_recv.at[i], sibling)

    def swap_out(i):
        at = jnp.where(i == 0, A_AT, B_AT)
        return remote(g.at[at, h], swapped.at[i], out_send.at[i], out_recv.at[i], partner)

    fixed_in = remote(x.at[A_AT, 0], x.at[FIXED, 0], fix_send, fix_recv, fixed_peer)
    fixed_out = remote(g.at[FIXED, 1 - q], extra, gfix_send, gfix_recv, fixed_peer)
    fixed_giver = both(is_fixed, even)
    fixed_taker = both(is_fixed, odd)

    def when(condition, action):
        @pl.when(condition)
        def _():
            action()

    share, items = x.shape[2], x.shape[3]
    groups = items // LANES

    def rows_of(block, group):
        return pl.ds(2 * group + block, share, stride=2 * groups)

    def take(source, block, at, half):
        for group in range(groups):
            x[at, half, :, pl.ds(group * LANES, LANES)] = source[rows_of(block, group), :]

    def give(block, value):
        for group in range(groups):
            out[rows_of(block, group), :] = value[:, group * LANES : (group + 1) * LANES]

    when(either(same, fixed_taker), own.start)
    for k in range(4):
        counts_in(k).start()

    barrier = pltpu.get_barrier_semaphore()
    peers = [
        (None, sibling), (None, right), (c > 0, left), (other, partner), (is_fixed, fixed_peer),
        *[(f[0], f[1]) for f in far], from_a3[:2], from_b3[:2], from_b4[:2],
    ]
    greeted = 0
    for condition, to in peers:
        def greet(to=to):
            pl.semaphore_signal(barrier, inc=1, device_id=to, device_id_type=MESH)

        if condition is None:
            greet()
            greeted += 1
        else:
            when(condition, greet)
            greeted += jnp.where(condition, 1, 0)
    pl.semaphore_wait(barrier, greeted)

    when(other, swap_in.start)

    @pl.loop(0, SLOTS)
    def _(at):
        g[at] = jnp.zeros_like(g[at])

    when(either(same, fixed_taker), own.wait)
    for source, condition in ((mine, same), (raw, other)):
        @pl.when(condition)
        def _(source=source):
            if source is raw:
                swap_in.wait_recv()
            for block in range(2):
                take(source, block, jnp.where(q == block, A_AT, B_AT), h)

    when(has_down_b, chain_b(0).start)
    when(has_down_a, chain_a(0).start)
    to_core(B_AT).start()
    to_core(A_AT).start()
    for i in (1, 0, 2, 3):
        when(far[i][0], far_block(i).start)
    when(fixed_giver, fixed_in.start)

    @pl.when(fixed_taker)
    def _():
        take(mine, 0, FIXED, 1)
        fixed_in.wait_recv()

    def meeting(k):
        a, b = slot_a(k), slot_b(k + differs)
        upper = jnp.where(is_fixed, jnp.where(even, A_AT, FIXED), jnp.where(even, a, b))
        lower = jnp.where(even, b, a)
        g_upper = jnp.where(is_fixed, FIXED, upper)
        counts_in(k).wait()
        for half in range(2):
            uh[half], ul[half] = split(x[upper, half])
            lh[half], ll[half] = split(x[lower, half])

        for start in range(0, items, tile):
            rows = pl.ds(start, tile)
            scores = 0.0
            for half in range(2):
                scores += dot3((uh[half, :, rows], ul[half, :, rows]), (lh[half], ll[half]), ((0,), (0,)))
            r = split(residual_of(scores, tiles[k, rows, :]))
            for half in range(2):
                g[lower, half] += dot3((uh[half, :, rows], ul[half, :, rows]), r, ((1,), (0,)))
                g[g_upper, half, :, rows] += dot3((lh[half], ll[half]), r, ((1,), (1,)))

    has = {1: has_up_a, 2: has_up_a, 3: has_up_a, 5: has_up_b, 6: has_up_b, 7: has_b3, 8: has_b4}

    def pass_on(at, copy=None, condition=None):
        when(has[at], arrival(at).wait_recv)
        if copy is not None:
            when(condition, copy.start)
        when(has[at], to_core(at).start)

    def second_blocks():
        pass_on(B_AT + 2, chain_b(2), send_b2)
        pass_on(A_AT + 2, chain_a(2), send_a2)

    def far_blocks():
        pass_on(B_AT + 3, chain_b(3), send_b3)
        pass_on(A_AT + 3)
        pass_on(B_AT + 4)

    def other_half(at, condition=None):
        conditions = [i for i in (has.get(at), condition) if i is not None]
        if conditions:
            when(both(*conditions), from_core_arrival(at).wait_recv)
        else:
            from_core_arrival(at).wait_recv()

    def gathered(at):
        g_core(at).wait_recv()
        g[at, h] += from_core[at]

    def give_back(at, source, present, up):
        when(source[0], g_return(at, source).start)
        when(both(present, jnp.logical_not(source[0])), g_chain(at, up).start)

    def far_back():
        g_core(B_AT + 4).start()
        g_core(A_AT + 3).start()
        g_core(B_AT + 3).start()
        gathered(B_AT + 4)
        give_back(B_AT + 4, from_b4, has_b4, up_b)
        gathered(A_AT + 3)
        give_back(A_AT + 3, from_a3, has_up_a, up_a)
        gathered(B_AT + 3)

        @pl.when(send_b3)
        def _():
            g_chain_arrival(B_AT + 3).wait_recv()
            g[B_AT + 3, h] += from_chain[B_AT + 3]

        give_back(B_AT + 3, from_b3, has_b3, up_b)

    def in_turn(*ks):
        turn_at = ks[-1]
        for i in range(len(ks) - 2, -1, -1):
            turn_at = jnp.where(turn_now[0] == i, ks[i], turn_at)
        return turn_at

    near_same, near_other = both(near, same), both(near, other)
    plain_same, plain_other = both(plain, same), both(plain, other)
    turn_now = [0]
    order = (
        0,
        jnp.where(plain_other, 3, 1),
        jnp.where(plain_same, 3, 2),
        jnp.where(near, 3, jnp.where(same, 2, 1)),
    )

    @pl.loop(0, 4)
    def _(turn):
        turn_now[0] = turn

        @pl.when(turn == 0)
        def _():
            pass_on(B_AT + 1, chain_b(1), has_down_b)
            pass_on(A_AT + 1, chain_a(1), has_down_a)
            other_half(B_AT)
            other_half(A_AT)
            other_half(B_AT + 1, other)

        @pl.when(turn == 1)
        def _():
            when(near, second_blocks)
            when(plain, far_blocks)
            other_half(A_AT + 1, either(same, near))
            other_half(B_AT + 1, same)
            other_half(B_AT + 2, near_other)
            other_half(A_AT + 3, plain_other)
            other_half(B_AT + 3, plain_other)
            other_half(B_AT + 4, plain_other)

        @pl.when(turn == 2)
        def _():
            when(near, far_blocks)
            when(plain, second_blocks)
            other_half(A_AT + 3, plain_same)
            other_half(B_AT + 3, either(plain_same, near_other))
            other_half(A_AT + 2, either(other, alias_b, near))
            other_half(B_AT + 2, either(plain_other, near_same))

        @pl.when(turn == 3)
        def _():
            when(plain, far_back)
            other_half(A_AT + 1, plain_other)
            other_half(A_AT + 2, both(plain_same, jnp.logical_not(alias_b)))
            other_half(B_AT + 2, plain_same)
            other_half(A_AT + 3, near)
            other_half(B_AT + 3, near_same)
            other_half(B_AT + 4, near_other)

        meeting(in_turn(*order))

    when(near, far_back)
    for k in (2, 1, 0):
        g_core(A_AT + k).start()
        g_core(B_AT + k).start()
    when(is_fixed, fixed_out.start)

    def chained(at, alias, has_down):
        @pl.when(has_down)
        def _():
            g_chain_arrival(at).wait_recv()
            g[alias, h] += from_chain[at]

    def add_returned(i, at):
        @pl.when(far[i][0])
        def _():
            g_return_arrival(i).wait_recv()
            g[at, h] += returned[i]

    gathered(A_AT + 2)
    chained(A_AT + 2, slot_a(2), send_a2)
    when(has_up_a, g_chain(A_AT + 2, up_a).start)
    gathered(B_AT + 2)
    chained(B_AT + 2, slot_b(2), send_b2)
    when(has_up_b, g_chain(B_AT + 2, up_b).start)
    gathered(A_AT + 1)
    gathered(B_AT + 1)
    chained(A_AT + 1, slot_a(1), has_down_a)
    when(has_up_a, g_chain(A_AT + 1, up_a).start)
    chained(B_AT + 1, slot_b(1), has_down_b)
    when(has_up_b, g_chain(B_AT + 1, up_b).start)
    gathered(A_AT)
    gathered(B_AT)
    for i in (0, 1, 2, 3):
        add_returned(i, far[i][2])
    chained(A_AT, slot_a(0), has_down_a)

    @pl.when(other)
    def _():
        swap_out(0).start()

    @pl.when(same)
    def _():
        for block in range(2):
            when(q == block, functools.partial(lambda b: give(b, g[A_AT, h]), block))

    chained(B_AT, B_AT, has_down_b)

    @pl.when(other)
    def _():
        swap_out(1).start()
        swap_out(0).wait_recv()
        for block in range(2):
            when(q == 1 - block, functools.partial(lambda b: give(b, swapped[0]), block))
        swap_out(1).wait_recv()
        for block in range(2):
            when(q == block, functools.partial(lambda b: give(b, swapped[1]), block))

    @pl.when(same)
    def _():
        for block in range(2):
            when(q == 1 - block, functools.partial(lambda b: give(b, g[B_AT, h]), block))

    @pl.when(is_fixed)
    def _():
        fixed_out.wait_recv()
        for group in range(groups):
            lanes = pl.ds(group * LANES, LANES)
            out[rows_of(0, group), :] += g[FIXED, q, :, lanes] + extra[:, lanes]

    other_half(B_AT + 4, same)

    @pl.when(other)
    def _():
        swap_in.wait_send()
        swap_out(0).wait_send()
        swap_out(1).wait_send()

    when(fixed_giver, fixed_in.wait_send)
    when(is_fixed, fixed_out.wait_send)
    for i in range(4):
        when(far[i][0], far_block(i).wait_send)
    for k in range(2):
        when(has_down_a, chain_a(k).wait_send)
        when(has_down_b, chain_b(k).wait_send)
    when(send_a2, chain_a(2).wait_send)
    when(send_b2, chain_b(2).wait_send)
    when(send_b3, chain_b(3).wait_send)
    for at in range(9):
        if at in has:
            when(has[at], to_core(at).wait_send)
        else:
            to_core(at).wait_send()
        g_core(at).wait_send()
    for k in (1, 2):
        when(has_up_a, g_chain(A_AT + k, up_a).wait_send)
        when(has_up_b, g_chain(B_AT + k, up_b).wait_send)
    for at, source, present, up in (
        (A_AT + 3, from_a3, has_up_a, up_a), (B_AT + 3, from_b3, has_b3, up_b), (B_AT + 4, from_b4, has_b4, up_b),
    ):
        when(source[0], g_return(at, source).wait_send)
        when(both(present, jnp.logical_not(source[0])), g_chain(at, up).wait_send)


def solution(mesh):
    players = mesh.shape["blk"]
    chips = players // 2

    def body(factors, state, counts):
        share, items = factors.shape[2], factors.shape[3]
        tile = min(512, items)
        dma = pltpu.SemaphoreType.DMA
        packed = pack(factors[0])
        grad = pl.pallas_call(
            functools.partial(kernel, chips, tile),
            out_shape=jax.ShapeDtypeStruct(packed.shape, F32),
            in_specs=[pl.BlockSpec(memory_space=pl.ANY)] * 2,
            out_specs=pl.BlockSpec(memory_space=pltpu.VMEM),
            scratch_shapes=[
                pltpu.VMEM((SLOTS, 2, share, items), F32),
                pltpu.VMEM((SLOTS, 2, share, items), F32),
                pltpu.VMEM(packed.shape, F32),
                pltpu.VMEM(packed.shape, F32),
                pltpu.VMEM((9, share, items), F32),
                pltpu.VMEM((8, share, items), F32),
                pltpu.VMEM((4, share, items), F32),
                pltpu.VMEM((2, share, items), F32),
                pltpu.VMEM((share, items), F32),
                pltpu.VMEM((4, items, items), jnp.int32),
                pltpu.VMEM((2, share, items), BF16),
                pltpu.VMEM((2, share, items), BF16),
                pltpu.VMEM((2, share, items), BF16),
                pltpu.VMEM((2, share, items), BF16),
                dma((2,)), dma((4,)),
                dma, dma, dma, dma,
                dma((11,)), dma((9,)), dma((9,)), dma((9,)),
                dma((9,)), dma((9,)), dma((9,)), dma((8,)), dma((4,)),
                dma((2,)), dma((2,)), dma, dma,
            ],
            compiler_params=pltpu.CompilerParams(
                collective_id=0, has_side_effects=True, vmem_limit_bytes=60 * 1024 * 1024
            ),
        )(packed, counts[0])
        new_state = pack(state[0]) + grad * grad
        step = grad / jnp.sqrt(new_state)
        return (unpack(step, factors.shape), unpack(new_state, factors.shape))

    in_specs = (
        P("blk", None, "rep", None),
        P("blk", None, "rep", None),
        P("blk", None, None, None),
    )
    out_specs = (P("blk", None, "rep", None), P("blk", None, "rep", None))
    return jax.shard_map(body, mesh=mesh, in_specs=in_specs, out_specs=out_specs, check_vma=False)
```

```python
import functools

import jax
import jax.numpy as jnp
from jax import lax
from jax.experimental import pallas as pl
from jax.experimental.pallas import tpu as pltpu
from jax.sharding import PartitionSpec as P

MESH = pl.DeviceIdType.MESH
BF16 = jnp.bfloat16
F32 = jnp.float32
clip_bound = 2.0

A_AT, B_AT, FIXED, SLOTS = 0, 4, 9, 10
LANES = 128


def residual_of(scores, count_tile):
    amount = count_tile.astype(F32)
    present = count_tile > 0
    clamped = jnp.maximum(amount, 1.0)
    weight = 0.1 + 0.25 * jnp.sqrt(clamped)
    kept = weight * jnp.clip(scores - jnp.log(clamped), -clip_bound, clip_bound)
    return jnp.where(present, kept, 0.5 * jax.nn.sigmoid(scores))


def split(value):
    high = value.astype(BF16)
    return high, (value - high.astype(F32)).astype(BF16)


def product(left, right, dims):
    return lax.dot_general(left, right, (dims, ((), ())), preferred_element_type=F32)


def pack(blocks):
    two, share, items = blocks.shape
    return blocks.reshape(two, share, items // LANES, LANES).transpose(1, 2, 0, 3).reshape(-1, LANES)


def unpack(rows, dims):
    one, two, share, items = dims
    return rows.reshape(share, items // LANES, two, LANES).transpose(2, 0, 1, 3).reshape(dims)


def kernel(
    chips, factors, counts, out,
    x, g, raw, mine, from_core, from_chain, returned, swapped, extra, tiles, upper_parts, lower_parts, lower_twice,
    load_sem, count_sem,
    in_send, in_recv, fix_send, fix_recv,
    out_block_send, block_recv, core_send, core_recv,
    gcore_send, gcore_recv, gback_send, gchain_recv, returned_recv,
    out_send, out_recv, gfix_send, gfix_recv,
):
    p, q = lax.axis_index("blk"), lax.axis_index("rep")
    c, h = p // 2, p % 2
    differs = (h + q) % 2
    same = differs == 0
    other = differs == 1
    even, odd = q == 0, q == 1

    def both(*conditions):
        return functools.reduce(jnp.logical_and, conditions)

    def either(*conditions):
        return functools.reduce(jnp.logical_or, conditions)

    def pick(condition, a, b):
        return tuple(jnp.where(condition, i, j) for i, j in zip(a, b))

    def ahead(n):
        over = c + n >= chips
        return (jnp.where(over, 2 * chips - 1 - c - n, c + n) * 2 + h, jnp.where(over, 1 - q, q))

    def at_chip(chip):
        return (jnp.maximum(chip, 0) * 2 + h, q)

    sibling = (c * 2 + 1 - h, q)
    partner = (c * 2 + 1 - h, 1 - q)
    fixed_peer = (p, 1 - q)
    right, left = ahead(1), at_chip(c - 1)
    down_a, up_a = pick(even, right, left), pick(even, left, right)
    down_b, up_b = up_a, down_a
    has_up_a = either(odd, c > 0)
    has_down_a = either(even, c > 0)
    has_up_b, has_down_b = has_down_a, has_up_a
    alias_a, alias_b = both(even, c == 0), both(odd, c == 0)
    is_fixed = p == 0

    half_way = chips // 2

    def right_fed(chip):
        return both(chip > half_way, chip < half_way + 3)

    def left_fed(chip):
        return both(chip >= half_way - 3, chip < half_way - 1)

    def fed_a3(to):
        return jnp.where(to[1] == 0, right_fed(to[0] // 2), left_fed(to[0] // 2))

    def fed_b3(to):
        return jnp.where(to[1] == 0, left_fed(to[0] // 2), right_fed(to[0] // 2))

    def fed_b4(to):
        return both(to[1] == 0, to[0] // 2 == chips - 4)

    def home_of(to):
        stays = to[1] == h
        return (jnp.where(stays, to[0], to[0] // 2 * 2 + 1 - h), jnp.where(stays, to[1], 1 - to[1]))

    over = c + 1 >= chips
    partner_right = (jnp.where(over, c, c + 1) * 2 + 1 - h, jnp.where(over, q, 1 - q))
    partner_left = (jnp.maximum(c - 1, 0) * 2 + 1 - h, 1 - q)
    last_a_from, last_b_from = pick(odd, partner_right, partner_left), pick(odd, partner_left, partner_right)
    alias_home = both(odd, c == 0)
    here = (p, q)
    near = both(c >= half_way - 3, c < half_way + 3)
    plain = jnp.logical_not(near)
    send_a2, send_b2 = both(has_down_a, fed_a3(down_a)), both(has_down_b, fed_b3(down_b))
    send_b3 = both(has_down_b, fed_b4(down_b))

    has_b3, has_b4 = either(even, c >= 2), either(even, c >= 1)
    far_to = (
        pick(even, ahead(3), at_chip(jnp.where(c == 0, 2, c - 3))),
        pick(odd, ahead(3), at_chip(jnp.where(c >= 3, c - 3, 3 - c))),
        pick(odd, ahead(4), at_chip(c - 4)),
        at_chip(3 - c),
    )
    first_to_b, second_to_a = alias_b, both(even, c < 3)
    not_fed = (
        jnp.logical_not(jnp.where(first_to_b, fed_b3(far_to[0]), fed_a3(far_to[0]))),
        jnp.logical_not(jnp.where(second_to_a, fed_a3(far_to[1]), fed_b3(far_to[1]))),
        jnp.logical_not(fed_b4(far_to[2])),
    )
    far = (
        (both(either(even, c >= 3, c == 0), not_fed[0]), far_to[0],
         jnp.where(alias_a, B_AT, A_AT), jnp.where(first_to_b, B_AT + 3, A_AT + 3)),
        (both(either(odd, c >= 1), not_fed[1]), far_to[1],
         B_AT, jnp.where(second_to_a, A_AT + 3, B_AT + 3)),
        (both(either(odd, c >= 4), not_fed[2]), far_to[2], B_AT, B_AT + 4),
        (both(odd, c <= 2), far_to[3], A_AT, B_AT + 4),
    )
    from_a3 = (both(has_up_a, jnp.logical_not(fed_a3(here))), pick(even, at_chip(jnp.where(c >= 3, c - 3, 3 - c)), ahead(3)),
               jnp.where(both(even, c < 3), 1, 0))
    from_b3 = (both(has_b3, jnp.logical_not(fed_b3(here))), pick(even, ahead(3), at_chip(jnp.where(c >= 3, c - 3, 2 - c))),
               jnp.where(both(odd, c == 2), 0, 1))
    from_b4 = (both(has_b4, jnp.logical_not(fed_b4(here))), pick(even, ahead(4), at_chip(jnp.where(c >= 4, c - 4, 3 - c))),
               jnp.where(both(odd, c < 4), 3, 2))

    def slot_a(k):
        return jnp.where(alias_a, B_AT + k, A_AT + k)

    def slot_b(k):
        at = jnp.where(both(alias_b, k >= 1), A_AT + k - 1, B_AT + k)
        return jnp.where(both(odd, c == 1, k == 3), A_AT, at)

    def remote(src, dst, send, recv, to):
        return pltpu.make_async_remote_copy(
            src_ref=src, dst_ref=dst, send_sem=send, recv_sem=recv, device_id=to, device_id_type=MESH
        )

    own = pltpu.make_async_copy(factors, mine, load_sem.at[0])
    swap_in = remote(factors, raw, in_send, in_recv, partner)

    def counts_in(k):
        return pltpu.make_async_copy(counts.at[2 * k + differs], tiles.at[k], count_sem.at[k])

    def chain_a(k):
        to = A_AT + k + 1
        return remote(x.at[slot_a(k), h], x.at[to, h], out_block_send.at[4 + k], block_recv.at[to], down_a)

    def chain_b(k):
        to = B_AT + k + 1
        return remote(x.at[slot_b(k), h], x.at[to, h], out_block_send.at[7 + k], block_recv.at[to], down_b)

    def far_block(i):
        _, to, at, into = far[i]
        return remote(x.at[at, h], x.at[into, h], out_block_send.at[i], block_recv.at[into], to)

    def arrival(at):
        return remote(x.at[at, h], x.at[at, h], out_block_send.at[0], block_recv.at[at], sibling)

    def to_core(at):
        return remote(x.at[at, h], x.at[at, h], core_send.at[at], core_recv.at[at], sibling)

    def from_core_arrival(at):
        return remote(x.at[at, 1 - h], x.at[at, 1 - h], core_send.at[at], core_recv.at[at], sibling)

    def g_core(at):
        return remote(g.at[at, 1 - h], from_core.at[at], gcore_send.at[at], gcore_recv.at[at], sibling)

    def g_chain(at, to):
        return remote(g.at[at, h], from_chain.at[at - 1], gback_send.at[at], gchain_recv.at[at - 1], to)

    def g_chain_arrival(at):
        return remote(g.at[at, h], from_chain.at[at], gback_send.at[at], gchain_recv.at[at], sibling)

    def g_return(at, source):
        _, to, i = source
        return remote(g.at[at, h], returned.at[i], gback_send.at[at], returned_recv.at[i], to)

    def g_return_arrival(i):
        return remote(g.at[0, h], returned.at[i], gback_send.at[0], returned_recv.at[i], sibling)

    def swap_out(i):
        at = jnp.where(i == 0, A_AT, B_AT)
        return remote(g.at[at, h], swapped.at[i], out_send.at[i], out_recv.at[i], partner)

    fixed_in = remote(x.at[A_AT, 0], x.at[FIXED, 0], fix_send, fix_recv, fixed_peer)
    fixed_out = remote(g.at[FIXED, 1 - q], extra, gfix_send, gfix_recv, fixed_peer)
    fixed_giver = both(is_fixed, even)
    fixed_taker = both(is_fixed, odd)

    def when(condition, action):
        @pl.when(condition)
        def _():
            action()

    share, items = x.shape[2], x.shape[3]
    groups = items // LANES

    def rows_of(block, group):
        return pl.ds(2 * group + block, share, stride=2 * groups)

    def take(source, block, at, half):
        for group in range(groups):
            x[at, half, :, pl.ds(group * LANES, LANES)] = source[rows_of(block, group), :]

    def give(block, value):
        for group in range(groups):
            out[rows_of(block, group), :] = value[:, group * LANES : (group + 1) * LANES]

    when(either(same, fixed_taker), own.start)
    for k in range(4):
        counts_in(k).start()

    barrier = pltpu.get_barrier_semaphore()
    peers = [
        (None, sibling), (None, right), (c > 0, left), (other, partner), (is_fixed, fixed_peer),
        *[(f[0], f[1]) for f in far], from_a3[:2], from_b3[:2], from_b4[:2],
    ]
    greeted = 0
    for condition, to in ((both(other, has_up_a), last_a_from), (both(other, has_up_b), last_b_from)):
        @pl.when(condition)
        def _(to=to):
            pl.semaphore_signal(barrier, inc=1, device_id=to, device_id_type=MESH)

    for condition, up in ((has_up_a, up_a), (has_up_b, up_b)):
        greeted += jnp.where(both(condition, up[1] != h), 1, 0)
    for condition, to in peers:
        def greet(to=to):
            pl.semaphore_signal(barrier, inc=1, device_id=to, device_id_type=MESH)

        if condition is None:
            greet()
            greeted += 1
        else:
            when(condition, greet)
            greeted += jnp.where(condition, 1, 0)
    pl.semaphore_wait(barrier, greeted)

    when(other, swap_in.start)

    when(either(same, fixed_taker), own.wait)
    for source, condition in ((mine, same), (raw, other)):
        @pl.when(condition)
        def _(source=source):
            if source is raw:
                swap_in.wait_recv()
            for block in range(2):
                take(source, block, jnp.where(q == block, A_AT, B_AT), h)

    when(has_down_b, chain_b(0).start)
    when(has_down_a, chain_a(0).start)
    to_core(B_AT).start()
    to_core(A_AT).start()
    for i in (1, 0, 2, 3):
        when(far[i][0], far_block(i).start)
    when(fixed_giver, fixed_in.start)

    @pl.loop(0, SLOTS)
    def _(at):
        g[at] = jnp.zeros_like(g[at])

    padded = upper_parts.shape[0] // 4
    if padded > share:
        for parts in (upper_parts, lower_parts):
            for i in range(4):
                parts[pl.ds(i * padded + share, padded - share), :] = jnp.zeros((padded - share, items), BF16)

    @pl.when(fixed_taker)
    def _():
        take(mine, 0, FIXED, 1)
        fixed_in.wait_recv()

    def meeting(k):
        a, b = slot_a(k), slot_b(k + differs)
        upper = jnp.where(is_fixed, jnp.where(even, A_AT, FIXED), jnp.where(even, a, b))
        lower = jnp.where(even, b, a)
        g_upper = jnp.where(is_fixed, FIXED, upper)
        counts_in(k).wait()
        for parts, at in ((upper_parts, upper), (lower_parts, lower)):
            for half in range(2):
                high, low = split(x[at, half])
                parts[pl.ds(half * padded, share), :] = high
                parts[pl.ds((2 + half) * padded, share), :] = low
        lower_twice[: 2 * padded] = lower_parts[: 2 * padded]
        lower_twice[2 * padded :] = lower_parts[: 2 * padded]
        over_features = ((0,), (0,))
        scores = product(upper_parts[...], lower_twice[...], over_features) + product(
            upper_parts[: 2 * padded], lower_parts[2 * padded :], over_features
        )
        r_high, r_low = split(residual_of(scores, tiles[k]))

        def add_to(at, parts, dims):
            first = product(parts[...], r_high, dims)
            second = product(parts[: 2 * padded], r_low, dims)
            for half in range(2):
                i, j = half * padded, (2 + half) * padded
                g[at, half] += first[i : i + share] + first[j : j + share] + second[i : i + share]

        add_to(lower, upper_parts, ((1,), (0,)))
        add_to(g_upper, lower_parts, ((1,), (1,)))

    has = {1: has_up_a, 2: has_up_a, 3: has_up_a, 5: has_up_b, 6: has_up_b, 7: has_b3, 8: has_b4}

    def pass_on(at, copy=None, condition=None):
        when(has[at], arrival(at).wait_recv)
        if copy is not None:
            when(condition, copy.start)
        when(has[at], to_core(at).start)

    def second_blocks():
        pass_on(B_AT + 2, chain_b(2), send_b2)
        pass_on(A_AT + 2, chain_a(2), send_a2)

    def far_blocks():
        pass_on(B_AT + 3, chain_b(3), send_b3)
        pass_on(A_AT + 3)
        pass_on(B_AT + 4)

    def other_half(at, condition=None):
        conditions = [i for i in (has.get(at), condition) if i is not None]
        if conditions:
            when(both(*conditions), from_core_arrival(at).wait_recv)
        else:
            from_core_arrival(at).wait_recv()

    def gathered(at):
        g_core(at).wait_recv()
        g[at, h] += from_core[at]

    def give_back(at, source, present, up):
        when(source[0], g_return(at, source).start)
        when(both(present, jnp.logical_not(source[0])), g_chain(at, up).start)

    def far_back():
        g_core(B_AT + 4).start()
        g_core(A_AT + 3).start()
        g_core(B_AT + 3).start()
        gathered(B_AT + 4)
        give_back(B_AT + 4, from_b4, has_b4, up_b)
        gathered(A_AT + 3)
        give_back(A_AT + 3, from_a3, has_up_a, up_a)
        gathered(B_AT + 3)

        @pl.when(send_b3)
        def _():
            g_chain_arrival(B_AT + 3).wait_recv()
            g[B_AT + 3, h] += from_chain[B_AT + 3]

        give_back(B_AT + 3, from_b3, has_b3, up_b)

    def in_turn(*ks):
        turn_at = ks[-1]
        for i in range(len(ks) - 2, -1, -1):
            turn_at = jnp.where(turn_now[0] == i, ks[i], turn_at)
        return turn_at

    near_same, near_other = both(near, same), both(near, other)
    plain_same, plain_other = both(plain, same), both(plain, other)
    turn_now = [0]
    order = (
        0,
        jnp.where(plain_other, 3, 1),
        jnp.where(plain_same, 3, 2),
        jnp.where(near, 3, jnp.where(same, 2, 1)),
    )

    @pl.loop(0, 4)
    def _(turn):
        turn_now[0] = turn

        @pl.when(turn == 0)
        def _():
            pass_on(B_AT + 1, chain_b(1), has_down_b)
            pass_on(A_AT + 1, chain_a(1), has_down_a)
            other_half(B_AT)
            other_half(A_AT)
            other_half(B_AT + 1, other)

        @pl.when(turn == 1)
        def _():
            when(near, second_blocks)
            when(plain, far_blocks)
            other_half(A_AT + 1, either(same, near))
            other_half(B_AT + 1, same)
            other_half(B_AT + 2, near_other)
            other_half(A_AT + 3, plain_other)
            other_half(B_AT + 3, plain_other)
            other_half(B_AT + 4, plain_other)

        @pl.when(turn == 2)
        def _():
            when(near, far_blocks)
            when(plain, second_blocks)
            other_half(A_AT + 3, plain_same)
            other_half(B_AT + 3, either(plain_same, near_other))
            other_half(A_AT + 2, either(other, alias_b, near))
            other_half(B_AT + 2, either(plain_other, near_same))

        @pl.when(turn == 3)
        def _():
            when(plain, far_back)
            other_half(A_AT + 1, plain_other)
            other_half(A_AT + 2, both(plain_same, jnp.logical_not(alias_b)))
            other_half(B_AT + 2, plain_same)
            other_half(A_AT + 3, near)
            other_half(B_AT + 3, near_same)
            other_half(B_AT + 4, near_other)

        meeting(in_turn(*order))

    when(near, far_back)
    for k in (2, 1, 0):
        g_core(A_AT + k).start()
        g_core(B_AT + k).start()
    when(is_fixed, fixed_out.start)

    def chained(at, alias, has_down):
        @pl.when(has_down)
        def _():
            g_chain_arrival(at).wait_recv()
            g[alias, h] += from_chain[at]

    def add_returned(i, at):
        @pl.when(far[i][0])
        def _():
            g_return_arrival(i).wait_recv()
            g[at, h] += returned[i]

    gathered(A_AT + 2)
    chained(A_AT + 2, slot_a(2), send_a2)
    when(has_up_a, g_chain(A_AT + 2, up_a).start)
    gathered(B_AT + 2)
    chained(B_AT + 2, slot_b(2), send_b2)
    when(has_up_b, g_chain(B_AT + 2, up_b).start)
    gathered(A_AT)
    gathered(B_AT)
    chained(B_AT + 1, slot_b(1), alias_b)
    for i in (0, 1, 2, 3):
        add_returned(i, far[i][2])

    @pl.when(other)
    def _():
        swap_out(0).start()
        swap_out(1).start()

    gathered(A_AT + 1)
    gathered(B_AT + 1)
    chained(A_AT + 1, slot_a(1), has_down_a)
    when(has_up_a, g_chain(A_AT + 1, home_of(up_a)).start)
    chained(B_AT + 1, B_AT + 1, both(has_down_b, jnp.logical_not(alias_b)))
    when(has_up_b, g_chain(B_AT + 1, home_of(up_b)).start)
    @pl.when(other)
    def _():
        swap_out(0).wait_recv()
        swap_out(1).wait_recv()

        @pl.when(has_up_a)
        def _():
            g_chain_arrival(A_AT).wait_recv()
            swapped[jnp.where(alias_home, 1, 0)] += from_chain[A_AT]

        for block in range(2):
            when(q == 1 - block, functools.partial(lambda b: give(b, swapped[0]), block))

        @pl.when(has_up_b)
        def _():
            g_chain_arrival(B_AT).wait_recv()
            swapped[1] += from_chain[B_AT]

        for block in range(2):
            when(q == block, functools.partial(lambda b: give(b, swapped[1]), block))

    @pl.when(same)
    def _():
        chained(A_AT, slot_a(0), has_down_a)
        for block in range(2):
            when(q == block, functools.partial(lambda b: give(b, g[A_AT, h]), block))
        chained(B_AT, B_AT, has_down_b)
        for block in range(2):
            when(q == 1 - block, functools.partial(lambda b: give(b, g[B_AT, h]), block))

    @pl.when(is_fixed)
    def _():
        fixed_out.wait_recv()
        for group in range(groups):
            lanes = pl.ds(group * LANES, LANES)
            out[rows_of(0, group), :] += g[FIXED, q, :, lanes] + extra[:, lanes]

    other_half(B_AT + 4, same)

    @pl.when(other)
    def _():
        swap_in.wait_send()
        swap_out(0).wait_send()
        swap_out(1).wait_send()

    when(fixed_giver, fixed_in.wait_send)
    when(is_fixed, fixed_out.wait_send)
    for i in range(4):
        when(far[i][0], far_block(i).wait_send)
    for k in range(2):
        when(has_down_a, chain_a(k).wait_send)
        when(has_down_b, chain_b(k).wait_send)
    when(send_a2, chain_a(2).wait_send)
    when(send_b2, chain_b(2).wait_send)
    when(send_b3, chain_b(3).wait_send)
    for at in range(9):
        if at in has:
            when(has[at], to_core(at).wait_send)
        else:
            to_core(at).wait_send()
        g_core(at).wait_send()
    for k in (1, 2):
        when(has_up_a, g_chain(A_AT + k, home_of(up_a) if k == 1 else up_a).wait_send)
        when(has_up_b, g_chain(B_AT + k, home_of(up_b) if k == 1 else up_b).wait_send)
    for at, source, present, up in (
        (A_AT + 3, from_a3, has_up_a, up_a), (B_AT + 3, from_b3, has_b3, up_b), (B_AT + 4, from_b4, has_b4, up_b),
    ):
        when(source[0], g_return(at, source).wait_send)
        when(both(present, jnp.logical_not(source[0])), g_chain(at, up).wait_send)


def solution(mesh):
    players = mesh.shape["blk"]
    chips = players // 2

    def body(factors, state, counts):
        share, items = factors.shape[2], factors.shape[3]
        padded = -(-share // 16) * 16
        dma = pltpu.SemaphoreType.DMA
        packed = pack(factors[0])
        grad = pl.pallas_call(
            functools.partial(kernel, chips),
            out_shape=jax.ShapeDtypeStruct(packed.shape, F32),
            in_specs=[pl.BlockSpec(memory_space=pl.ANY)] * 2,
            out_specs=pl.BlockSpec(memory_space=pltpu.VMEM),
            scratch_shapes=[
                pltpu.VMEM((SLOTS, 2, share, items), F32),
                pltpu.VMEM((SLOTS, 2, share, items), F32),
                pltpu.VMEM(packed.shape, F32),
                pltpu.VMEM(packed.shape, F32),
                pltpu.VMEM((9, share, items), F32),
                pltpu.VMEM((8, share, items), F32),
                pltpu.VMEM((4, share, items), F32),
                pltpu.VMEM((2, share, items), F32),
                pltpu.VMEM((share, items), F32),
                pltpu.VMEM((4, items, items), jnp.int32),
                pltpu.VMEM((4 * padded, items), BF16),
                pltpu.VMEM((4 * padded, items), BF16),
                pltpu.VMEM((4 * padded, items), BF16),
                dma((2,)), dma((4,)),
                dma, dma, dma, dma,
                dma((11,)), dma((9,)), dma((9,)), dma((9,)),
                dma((9,)), dma((9,)), dma((9,)), dma((8,)), dma((4,)),
                dma((2,)), dma((2,)), dma, dma,
            ],
            compiler_params=pltpu.CompilerParams(
                collective_id=0, has_side_effects=True, vmem_limit_bytes=60 * 1024 * 1024
            ),
        )(packed, counts[0])
        new_state = pack(state[0]) + grad * grad
        step = grad / jnp.sqrt(new_state)
        return (unpack(step, factors.shape), unpack(new_state, factors.shape))

    in_specs = (
        P("blk", None, "rep", None),
        P("blk", None, "rep", None),
        P("blk", None, None, None),
    )
    out_specs = (P("blk", None, "rep", None), P("blk", None, "rep", None))
    return jax.shard_map(body, mesh=mesh, in_specs=in_specs, out_specs=out_specs, check_vma=False)
```

```python
import functools

import jax
import jax.numpy as jnp
from jax import lax
from jax.experimental import pallas as pl
from jax.experimental.pallas import tpu as pltpu
from jax.sharding import PartitionSpec as P

MESH = pl.DeviceIdType.MESH
BF16 = jnp.bfloat16
F32 = jnp.float32
clip_bound = 2.0

A_AT, B_AT, FIXED, SLOTS = 0, 4, 9, 10
LANES = 128


def residual_of(scores, count_tile):
    amount = count_tile.astype(F32)
    present = count_tile > 0
    clamped = jnp.maximum(amount, 1.0)
    weight = 0.1 + 0.25 * jnp.sqrt(clamped)
    kept = weight * jnp.clip(scores - jnp.log(clamped), -clip_bound, clip_bound)
    return jnp.where(present, kept, 0.5 * jax.nn.sigmoid(scores))


def split(value):
    high = value.astype(BF16)
    return high, (value - high.astype(F32)).astype(BF16)


def product(left, right, dims):
    return lax.dot_general(left, right, (dims, ((), ())), preferred_element_type=F32)


def pack(blocks):
    two, share, items = blocks.shape
    return blocks.reshape(two, share, items // LANES, LANES).transpose(1, 2, 0, 3).reshape(-1, LANES)


def unpack(rows, dims):
    one, two, share, items = dims
    return rows.reshape(share, items // LANES, two, LANES).transpose(2, 0, 1, 3).reshape(dims)


def kernel(
    chips, factors, counts, out,
    x, g, raw, mine, spare, from_core, from_chain, returned, swapped, extra, tiles, upper_parts, lower_parts, lower_twice,
    load_sem, count_sem,
    in_send, in_recv, fix_send, fix_recv, hold_send,
    out_block_send, block_recv, core_send, core_recv,
    gcore_send, gcore_recv, gback_send, gchain_recv, returned_recv,
    out_send, out_recv, gfix_send, gfix_recv,
):
    p, q = lax.axis_index("blk"), lax.axis_index("rep")
    c, h = p // 2, p % 2
    differs = (h + q) % 2
    same = differs == 0
    other = differs == 1
    even, odd = q == 0, q == 1

    def both(*conditions):
        return functools.reduce(jnp.logical_and, conditions)

    def either(*conditions):
        return functools.reduce(jnp.logical_or, conditions)

    def pick(condition, a, b):
        return tuple(jnp.where(condition, i, j) for i, j in zip(a, b))

    def ahead(n):
        over = c + n >= chips
        return (jnp.where(over, 2 * chips - 1 - c - n, c + n) * 2 + h, jnp.where(over, 1 - q, q))

    def at_chip(chip):
        return (jnp.maximum(chip, 0) * 2 + h, q)

    sibling = (c * 2 + 1 - h, q)
    partner = (c * 2 + 1 - h, 1 - q)
    fixed_peer = (p, 1 - q)
    right, left = ahead(1), at_chip(c - 1)
    down_a, up_a = pick(even, right, left), pick(even, left, right)
    down_b, up_b = up_a, down_a
    has_up_a = either(odd, c > 0)
    has_down_a = either(even, c > 0)
    has_up_b, has_down_b = has_down_a, has_up_a
    alias_a, alias_b = both(even, c == 0), both(odd, c == 0)
    is_fixed = p == 0

    half_way = chips // 2

    def right_fed(chip):
        return both(chip > half_way, chip < half_way + 3)

    def left_fed(chip):
        return both(chip >= half_way - 3, chip < half_way - 1)

    def fed_a3(to):
        return jnp.where(to[1] == 0, right_fed(to[0] // 2), left_fed(to[0] // 2))

    def fed_b3(to):
        return jnp.where(to[1] == 0, left_fed(to[0] // 2), right_fed(to[0] // 2))

    def fed_b4(to):
        return both(to[1] == 0, to[0] // 2 == chips - 4)

    def home_of(to):
        stays = to[1] == h
        return (jnp.where(stays, to[0], to[0] // 2 * 2 + 1 - h), jnp.where(stays, to[1], 1 - to[1]))

    over = c + 1 >= chips
    partner_right = (jnp.where(over, c, c + 1) * 2 + 1 - h, jnp.where(over, q, 1 - q))
    partner_left = (jnp.maximum(c - 1, 0) * 2 + 1 - h, 1 - q)
    last_a_from, last_b_from = pick(odd, partner_right, partner_left), pick(odd, partner_left, partner_right)
    alias_home = both(odd, c == 0)
    here = (p, q)
    near = both(c >= half_way - 3, c < half_way + 3)
    plain = jnp.logical_not(near)
    send_a2, send_b2 = both(has_down_a, fed_a3(down_a)), both(has_down_b, fed_b3(down_b))
    send_b3 = both(has_down_b, fed_b4(down_b))

    has_b3, has_b4 = either(even, c >= 2), either(even, c >= 1)
    far_to = (
        pick(even, ahead(3), at_chip(jnp.where(c == 0, 2, c - 3))),
        pick(odd, ahead(3), at_chip(jnp.where(c >= 3, c - 3, 3 - c))),
        pick(odd, ahead(4), at_chip(c - 4)),
        at_chip(3 - c),
    )
    first_to_b, second_to_a = alias_b, both(even, c < 3)
    not_fed = (
        jnp.logical_not(jnp.where(first_to_b, fed_b3(far_to[0]), fed_a3(far_to[0]))),
        jnp.logical_not(jnp.where(second_to_a, fed_a3(far_to[1]), fed_b3(far_to[1]))),
        jnp.logical_not(fed_b4(far_to[2])),
    )
    far = (
        (both(either(even, c >= 3, c == 0), not_fed[0]), far_to[0],
         jnp.where(alias_a, B_AT, A_AT), jnp.where(first_to_b, B_AT + 3, A_AT + 3)),
        (both(either(odd, c >= 1), not_fed[1]), far_to[1],
         B_AT, jnp.where(second_to_a, A_AT + 3, B_AT + 3)),
        (both(either(odd, c >= 4), not_fed[2]), far_to[2], B_AT, B_AT + 4),
        (both(odd, c <= 2), far_to[3], A_AT, B_AT + 4),
    )
    from_a3 = (both(has_up_a, jnp.logical_not(fed_a3(here))), pick(even, at_chip(jnp.where(c >= 3, c - 3, 3 - c)), ahead(3)),
               jnp.where(both(even, c < 3), 1, 0))
    from_b3 = (both(has_b3, jnp.logical_not(fed_b3(here))), pick(even, ahead(3), at_chip(jnp.where(c >= 3, c - 3, 2 - c))),
               jnp.where(both(odd, c == 2), 0, 1))
    from_b4 = (both(has_b4, jnp.logical_not(fed_b4(here))), pick(even, ahead(4), at_chip(jnp.where(c >= 4, c - 4, 3 - c))),
               jnp.where(both(odd, c < 4), 3, 2))

    def slot_a(k):
        return jnp.where(alias_a, B_AT + k, A_AT + k)

    def slot_b(k):
        at = jnp.where(both(alias_b, k >= 1), A_AT + k - 1, B_AT + k)
        return jnp.where(both(odd, c == 1, k == 3), A_AT, at)

    def remote(src, dst, send, recv, to):
        return pltpu.make_async_remote_copy(
            src_ref=src, dst_ref=dst, send_sem=send, recv_sem=recv, device_id=to, device_id_type=MESH
        )

    own = pltpu.make_async_copy(factors, mine, load_sem.at[0])
    swap_in = remote(factors, raw, in_send, in_recv, partner)

    def counts_in(k):
        return pltpu.make_async_copy(counts.at[2 * k + differs], tiles.at[k], count_sem.at[k])

    def chain_a(k):
        to = A_AT + k + 1
        return remote(x.at[slot_a(k), h], x.at[to, h], out_block_send.at[4 + k], block_recv.at[to], down_a)

    def chain_b(k):
        to = B_AT + k + 1
        return remote(x.at[slot_b(k), h], x.at[to, h], out_block_send.at[7 + k], block_recv.at[to], down_b)

    def far_block(i):
        _, to, at, into = far[i]
        return remote(x.at[at, h], x.at[into, h], out_block_send.at[i], block_recv.at[into], to)

    def arrival(at):
        return remote(x.at[at, h], x.at[at, h], out_block_send.at[0], block_recv.at[at], sibling)

    def to_core(at):
        return remote(x.at[at, h], x.at[at, h], core_send.at[at], core_recv.at[at], sibling)

    def from_core_arrival(at):
        return remote(x.at[at, 1 - h], x.at[at, 1 - h], core_send.at[at], core_recv.at[at], sibling)

    holder = both(other, c >= chips - 4)

    def held(j):
        slot = (jnp.where(odd, A_AT + 1, B_AT + 1), jnp.where(odd, A_AT + 3, B_AT + 3), B_AT + 4)[j]
        chip = (c, 2 * chips - 4 - c, 2 * chips - 5 - c)[j]
        to = (jnp.clip(chip, 0, chips - 1) * 2 + 1 - h, q)
        return remote(spare, x.at[slot, 1 - h], hold_send.at[j], block_recv.at[slot], to)

    holds = (
        both(holder, c == chips - 1),
        both(holder, c >= chips - 3),
        both(holder, even, c <= chips - 2),
    )
    takes_held = (
        (both(same, c >= chips - 3), (jnp.clip(2 * chips - 4 - c, 0, chips - 1) * 2 + 1 - h, q)),
        (both(same, even, c >= chips - 3), (jnp.clip(2 * chips - 5 - c, 0, chips - 1) * 2 + 1 - h, q)),
    )

    def sends(condition, to):
        return both(condition, jnp.logical_not(both(other, to[1] != q)))

    def g_core(at):
        return remote(g.at[at, 1 - h], from_core.at[at], gcore_send.at[at], gcore_recv.at[at], sibling)

    def g_chain(at, to):
        return remote(g.at[at, h], from_chain.at[at - 1], gback_send.at[at], gchain_recv.at[at - 1], to)

    def g_chain_arrival(at):
        return remote(g.at[at, h], from_chain.at[at], gback_send.at[at], gchain_recv.at[at], sibling)

    def g_return(at, source):
        _, to, i = source
        return remote(g.at[at, h], returned.at[i], gback_send.at[at], returned_recv.at[i], to)

    def g_return_arrival(i):
        return remote(g.at[0, h], returned.at[i], gback_send.at[0], returned_recv.at[i], sibling)

    def swap_out(i):
        at = jnp.where(i == 0, A_AT, B_AT)
        return remote(g.at[at, h], swapped.at[i], out_send.at[i], out_recv.at[i], partner)

    fixed_in = remote(x.at[A_AT, 0], x.at[FIXED, 0], fix_send, fix_recv, fixed_peer)
    fixed_out = remote(g.at[FIXED, 1 - q], extra, gfix_send, gfix_recv, fixed_peer)
    fixed_giver = both(is_fixed, even)
    fixed_taker = both(is_fixed, odd)

    def when(condition, action):
        @pl.when(condition)
        def _():
            action()

    share, items = x.shape[2], x.shape[3]
    groups = items // LANES

    def rows_of(block, group):
        return pl.ds(2 * group + block, share, stride=2 * groups)

    def take(source, block, at, half):
        for group in range(groups):
            x[at, half, :, pl.ds(group * LANES, LANES)] = source[rows_of(block, group), :]

    def give(block, value):
        for group in range(groups):
            out[rows_of(block, group), :] = value[:, group * LANES : (group + 1) * LANES]

    when(either(same, fixed_taker, holder), own.start)
    for k in range(4):
        counts_in(k).start()

    barrier = pltpu.get_barrier_semaphore()
    peers = [
        (None, sibling), (None, right), (c > 0, left), (other, partner), (is_fixed, fixed_peer),
        *[(f[0], f[1]) for f in far], from_a3[:2], from_b3[:2], from_b4[:2],
    ]
    greeted = 0
    for condition, to in ((both(other, has_up_a), last_a_from), (both(other, has_up_b), last_b_from)):
        @pl.when(condition)
        def _(to=to):
            pl.semaphore_signal(barrier, inc=1, device_id=to, device_id_type=MESH)

    for condition, to in takes_held:
        @pl.when(condition)
        def _(to=to):
            pl.semaphore_signal(barrier, inc=1, device_id=to, device_id_type=MESH)

    greeted += jnp.where(holds[1], 1, 0) + jnp.where(holds[2], 1, 0)
    for condition, up in ((has_up_a, up_a), (has_up_b, up_b)):
        greeted += jnp.where(both(condition, up[1] != h), 1, 0)
    for condition, to in peers:
        def greet(to=to):
            pl.semaphore_signal(barrier, inc=1, device_id=to, device_id_type=MESH)

        if condition is None:
            greet()
            greeted += 1
        else:
            when(condition, greet)
            greeted += jnp.where(condition, 1, 0)
    pl.semaphore_wait(barrier, greeted)

    when(other, swap_in.start)

    when(either(same, fixed_taker, holder), own.wait)

    @pl.when(holder)
    def _():
        for group in range(groups):
            spare[:, pl.ds(group * LANES, LANES)] = mine[rows_of(0, group), :]
        for j in range(3):
            when(holds[j], held(j).start)

    for source, condition in ((mine, same), (raw, other)):
        @pl.when(condition)
        def _(source=source):
            if source is raw:
                swap_in.wait_recv()
            for block in range(2):
                take(source, block, jnp.where(q == block, A_AT, B_AT), h)

    when(sends(has_down_b, down_b), chain_b(0).start)
    when(sends(has_down_a, down_a), chain_a(0).start)
    to_core(B_AT).start()
    to_core(A_AT).start()
    def crossing(to):
        return (to[0] // 2 >= half_way) != (c >= half_way)

    def send_far(late):
        for i in (1, 0, 2, 3):
            crosses = crossing(far[i][1])
            when(both(sends(*far[i][:2]), crosses if late else jnp.logical_not(crosses)), far_block(i).start)

    send_far(False)
    when(fixed_giver, fixed_in.start)

    @pl.loop(0, SLOTS)
    def _(at):
        g[at] = jnp.zeros_like(g[at])

    padded = upper_parts.shape[0] // 4
    if padded > share:
        for parts in (upper_parts, lower_parts):
            for i in range(4):
                parts[pl.ds(i * padded + share, padded - share), :] = jnp.zeros((padded - share, items), BF16)

    @pl.when(fixed_taker)
    def _():
        take(mine, 0, FIXED, 1)
        fixed_in.wait_recv()

    def meeting(k):
        a, b = slot_a(k), slot_b(k + differs)
        upper = jnp.where(is_fixed, jnp.where(even, A_AT, FIXED), jnp.where(even, a, b))
        lower = jnp.where(even, b, a)
        g_upper = jnp.where(is_fixed, FIXED, upper)
        counts_in(k).wait()
        for parts, at in ((upper_parts, upper), (lower_parts, lower)):
            for half in range(2):
                high, low = split(x[at, half])
                parts[pl.ds(half * padded, share), :] = high
                parts[pl.ds((2 + half) * padded, share), :] = low
        lower_twice[: 2 * padded] = lower_parts[: 2 * padded]
        lower_twice[2 * padded :] = lower_parts[: 2 * padded]
        over_features = ((0,), (0,))
        scores = product(upper_parts[...], lower_twice[...], over_features) + product(
            upper_parts[: 2 * padded], lower_parts[2 * padded :], over_features
        )
        r_high, r_low = split(residual_of(scores, tiles[k]))

        def add_to(at, parts, dims):
            first = product(parts[...], r_high, dims)
            second = product(parts[: 2 * padded], r_low, dims)
            for half in range(2):
                i, j = half * padded, (2 + half) * padded
                g[at, half] += first[i : i + share] + first[j : j + share] + second[i : i + share]

        add_to(lower, upper_parts, ((1,), (0,)))
        add_to(g_upper, lower_parts, ((1,), (1,)))

    has = {1: has_up_a, 2: has_up_a, 3: has_up_a, 5: has_up_b, 6: has_up_b, 7: has_b3, 8: has_b4}

    def pass_on(at, copy=None, condition=None):
        when(has[at], arrival(at).wait_recv)
        if copy is not None:
            when(condition, copy.start)
        when(has[at], to_core(at).start)

    def second_blocks():
        pass_on(B_AT + 2, chain_b(2), send_b2)
        pass_on(A_AT + 2, chain_a(2), send_a2)

    def far_blocks():
        pass_on(B_AT + 3, chain_b(3), send_b3)
        pass_on(A_AT + 3)
        pass_on(B_AT + 4)

    def other_half(at, condition=None):
        conditions = [i for i in (has.get(at), condition) if i is not None]
        if conditions:
            when(both(*conditions), from_core_arrival(at).wait_recv)
        else:
            from_core_arrival(at).wait_recv()

    def gathered(at):
        g_core(at).wait_recv()
        g[at, h] += from_core[at]

    def give_back(at, source, present, up):
        when(source[0], g_return(at, source).start)
        when(both(present, jnp.logical_not(source[0])), g_chain(at, up).start)

    def far_back():
        g_core(B_AT + 4).start()
        g_core(A_AT + 3).start()
        g_core(B_AT + 3).start()
        gathered(B_AT + 4)
        give_back(B_AT + 4, from_b4, has_b4, up_b)
        gathered(A_AT + 3)
        give_back(A_AT + 3, from_a3, has_up_a, up_a)
        gathered(B_AT + 3)

        @pl.when(send_b3)
        def _():
            g_chain_arrival(B_AT + 3).wait_recv()
            g[B_AT + 3, h] += from_chain[B_AT + 3]

        give_back(B_AT + 3, from_b3, has_b3, up_b)

    def in_turn(*ks):
        turn_at = ks[-1]
        for i in range(len(ks) - 2, -1, -1):
            turn_at = jnp.where(turn_now[0] == i, ks[i], turn_at)
        return turn_at

    near_same, near_other = both(near, same), both(near, other)
    plain_same, plain_other = both(plain, same), both(plain, other)
    turn_now = [0]
    order = (
        0,
        jnp.where(plain_other, 3, 1),
        jnp.where(plain_same, 3, 2),
        jnp.where(near, 3, jnp.where(same, 2, 1)),
    )

    @pl.loop(0, 4)
    def _(turn):
        turn_now[0] = turn

        @pl.when(turn == 0)
        def _():
            pass_on(B_AT + 1, chain_b(1), has_down_b)
            pass_on(A_AT + 1, chain_a(1), has_down_a)
            other_half(B_AT)
            other_half(A_AT)
            send_far(True)
            other_half(B_AT + 1, other)

        @pl.when(turn == 1)
        def _():
            when(near, second_blocks)
            when(plain, far_blocks)
            other_half(A_AT + 1, either(same, near))
            other_half(B_AT + 1, same)
            other_half(B_AT + 2, near_other)
            other_half(A_AT + 3, plain_other)
            other_half(B_AT + 3, plain_other)
            other_half(B_AT + 4, plain_other)

        @pl.when(turn == 2)
        def _():
            when(near, far_blocks)
            when(plain, second_blocks)
            other_half(A_AT + 3, plain_same)
            other_half(B_AT + 3, either(plain_same, near_other))
            other_half(A_AT + 2, either(other, alias_b, near))
            other_half(B_AT + 2, either(plain_other, near_same))

        @pl.when(turn == 3)
        def _():
            when(plain, far_back)
            other_half(A_AT + 1, plain_other)
            other_half(A_AT + 2, both(plain_same, jnp.logical_not(alias_b)))
            other_half(B_AT + 2, plain_same)
            other_half(A_AT + 3, near)
            other_half(B_AT + 3, near_same)
            other_half(B_AT + 4, near_other)

        meeting(in_turn(*order))

    when(near, far_back)
    for k in (2, 1, 0):
        g_core(A_AT + k).start()
        g_core(B_AT + k).start()
    when(is_fixed, fixed_out.start)

    def chained(at, alias, has_down):
        @pl.when(has_down)
        def _():
            g_chain_arrival(at).wait_recv()
            g[alias, h] += from_chain[at]

    def add_returned(i, at):
        @pl.when(far[i][0])
        def _():
            g_return_arrival(i).wait_recv()
            g[at, h] += returned[i]

    gathered(A_AT + 2)
    chained(A_AT + 2, slot_a(2), send_a2)
    when(has_up_a, g_chain(A_AT + 2, up_a).start)
    gathered(B_AT + 2)
    chained(B_AT + 2, slot_b(2), send_b2)
    when(has_up_b, g_chain(B_AT + 2, up_b).start)
    gathered(A_AT)
    gathered(B_AT)
    chained(B_AT + 1, slot_b(1), alias_b)
    for i in (0, 1, 2, 3):
        add_returned(i, far[i][2])

    @pl.when(other)
    def _():
        swap_out(0).start()
        swap_out(1).start()

    gathered(A_AT + 1)
    gathered(B_AT + 1)
    chained(A_AT + 1, slot_a(1), has_down_a)
    when(has_up_a, g_chain(A_AT + 1, home_of(up_a)).start)
    chained(B_AT + 1, B_AT + 1, both(has_down_b, jnp.logical_not(alias_b)))
    when(has_up_b, g_chain(B_AT + 1, home_of(up_b)).start)
    @pl.when(other)
    def _():
        swap_out(0).wait_recv()
        swap_out(1).wait_recv()

        @pl.when(has_up_a)
        def _():
            g_chain_arrival(A_AT).wait_recv()
            swapped[jnp.where(alias_home, 1, 0)] += from_chain[A_AT]

        for block in range(2):
            when(q == 1 - block, functools.partial(lambda b: give(b, swapped[0]), block))

        @pl.when(has_up_b)
        def _():
            g_chain_arrival(B_AT).wait_recv()
            swapped[1] += from_chain[B_AT]

        for block in range(2):
            when(q == block, functools.partial(lambda b: give(b, swapped[1]), block))

    @pl.when(same)
    def _():
        chained(A_AT, slot_a(0), has_down_a)
        for block in range(2):
            when(q == block, functools.partial(lambda b: give(b, g[A_AT, h]), block))
        chained(B_AT, B_AT, has_down_b)
        for block in range(2):
            when(q == 1 - block, functools.partial(lambda b: give(b, g[B_AT, h]), block))

    @pl.when(is_fixed)
    def _():
        fixed_out.wait_recv()
        for group in range(groups):
            lanes = pl.ds(group * LANES, LANES)
            out[rows_of(0, group), :] += g[FIXED, q, :, lanes] + extra[:, lanes]

    other_half(B_AT + 4, same)

    @pl.when(other)
    def _():
        swap_in.wait_send()
        swap_out(0).wait_send()
        swap_out(1).wait_send()

    when(fixed_giver, fixed_in.wait_send)
    for j in range(3):
        when(holds[j], held(j).wait_send)
    when(is_fixed, fixed_out.wait_send)
    for i in range(4):
        when(sends(*far[i][:2]), far_block(i).wait_send)
    for k in range(2):
        when(sends(has_down_a, down_a) if k == 0 else has_down_a, chain_a(k).wait_send)
        when(sends(has_down_b, down_b) if k == 0 else has_down_b, chain_b(k).wait_send)
    when(send_a2, chain_a(2).wait_send)
    when(send_b2, chain_b(2).wait_send)
    when(send_b3, chain_b(3).wait_send)
    for at in range(9):
        if at in has:
            when(has[at], to_core(at).wait_send)
        else:
            to_core(at).wait_send()
        g_core(at).wait_send()
    for k in (1, 2):
        when(has_up_a, g_chain(A_AT + k, home_of(up_a) if k == 1 else up_a).wait_send)
        when(has_up_b, g_chain(B_AT + k, home_of(up_b) if k == 1 else up_b).wait_send)
    for at, source, present, up in (
        (A_AT + 3, from_a3, has_up_a, up_a), (B_AT + 3, from_b3, has_b3, up_b), (B_AT + 4, from_b4, has_b4, up_b),
    ):
        when(source[0], g_return(at, source).wait_send)
        when(both(present, jnp.logical_not(source[0])), g_chain(at, up).wait_send)


def solution(mesh):
    players = mesh.shape["blk"]
    chips = players // 2

    def body(factors, state, counts):
        share, items = factors.shape[2], factors.shape[3]
        padded = -(-share // 16) * 16
        dma = pltpu.SemaphoreType.DMA
        packed = pack(factors[0])
        grad = pl.pallas_call(
            functools.partial(kernel, chips),
            out_shape=jax.ShapeDtypeStruct(packed.shape, F32),
            in_specs=[pl.BlockSpec(memory_space=pl.ANY)] * 2,
            out_specs=pl.BlockSpec(memory_space=pltpu.VMEM),
            scratch_shapes=[
                pltpu.VMEM((SLOTS, 2, share, items), F32),
                pltpu.VMEM((SLOTS, 2, share, items), F32),
                pltpu.VMEM(packed.shape, F32),
                pltpu.VMEM(packed.shape, F32),
                pltpu.VMEM((share, items), F32),
                pltpu.VMEM((9, share, items), F32),
                pltpu.VMEM((8, share, items), F32),
                pltpu.VMEM((4, share, items), F32),
                pltpu.VMEM((2, share, items), F32),
                pltpu.VMEM((share, items), F32),
                pltpu.VMEM((4, items, items), jnp.int32),
                pltpu.VMEM((4 * padded, items), BF16),
                pltpu.VMEM((4 * padded, items), BF16),
                pltpu.VMEM((4 * padded, items), BF16),
                dma((2,)), dma((4,)),
                dma, dma, dma, dma, dma((3,)),
                dma((11,)), dma((9,)), dma((9,)), dma((9,)),
                dma((9,)), dma((9,)), dma((9,)), dma((8,)), dma((4,)),
                dma((2,)), dma((2,)), dma, dma,
            ],
            compiler_params=pltpu.CompilerParams(
                collective_id=0, has_side_effects=True, vmem_limit_bytes=60 * 1024 * 1024
            ),
        )(packed, counts[0])
        new_state = pack(state[0]) + grad * grad
        step = grad / jnp.sqrt(new_state)
        return (unpack(step, factors.shape), unpack(new_state, factors.shape))

    in_specs = (
        P("blk", None, "rep", None),
        P("blk", None, "rep", None),
        P("blk", None, None, None),
    )
    out_specs = (P("blk", None, "rep", None), P("blk", None, "rep", None))
    return jax.shard_map(body, mesh=mesh, in_specs=in_specs, out_specs=out_specs, check_vma=False)
```

```python
import functools

import jax
import jax.numpy as jnp
from jax import lax
from jax.experimental import pallas as pl
from jax.experimental.pallas import tpu as pltpu
from jax.sharding import PartitionSpec as P

MESH = pl.DeviceIdType.MESH
BF16 = jnp.bfloat16
F32 = jnp.float32
clip_bound = 2.0

A_AT, B_AT, FIXED, SLOTS = 0, 4, 9, 10
LANES = 128


def residual_of(scores, count_tile):
    amount = count_tile.astype(F32)
    present = count_tile > 0
    clamped = jnp.maximum(amount, 1.0)
    weight = 0.1 + 0.25 * jnp.sqrt(clamped)
    kept = weight * jnp.clip(scores - jnp.log(clamped), -clip_bound, clip_bound)
    return jnp.where(present, kept, 0.5 * jax.nn.sigmoid(scores))


def split(value):
    high = value.astype(BF16)
    return high, (value - high.astype(F32)).astype(BF16)


def product(left, right, dims):
    return lax.dot_general(left, right, (dims, ((), ())), preferred_element_type=F32)


def pack(blocks):
    two, share, items = blocks.shape
    return blocks.reshape(two, share, items // LANES, LANES).transpose(1, 2, 0, 3).reshape(-1, LANES)


def unpack(rows, dims):
    one, two, share, items = dims
    return rows.reshape(share, items // LANES, two, LANES).transpose(2, 0, 1, 3).reshape(dims)


def kernel(
    chips, factors, counts, out,
    x, g, raw, mine, spare, from_core, from_chain, returned, swapped, extra, tiles, upper_parts, lower_parts, lower_twice,
    load_sem, count_sem,
    in_send, in_recv, fix_send, fix_recv, hold_send,
    out_block_send, block_recv, core_send, core_recv,
    gcore_send, gcore_recv, gback_send, gchain_recv, returned_recv,
    out_send, out_recv, gfix_send, gfix_recv,
):
    p, q = lax.axis_index("blk"), lax.axis_index("rep")
    c, h = p // 2, p % 2
    differs = (h + q) % 2
    same = differs == 0
    other = differs == 1
    even, odd = q == 0, q == 1

    def both(*conditions):
        return functools.reduce(jnp.logical_and, conditions)

    def either(*conditions):
        return functools.reduce(jnp.logical_or, conditions)

    def pick(condition, a, b):
        return tuple(jnp.where(condition, i, j) for i, j in zip(a, b))

    def ahead(n):
        over = c + n >= chips
        return (jnp.where(over, 2 * chips - 1 - c - n, c + n) * 2 + h, jnp.where(over, 1 - q, q))

    def at_chip(chip):
        return (jnp.maximum(chip, 0) * 2 + h, q)

    sibling = (c * 2 + 1 - h, q)
    partner = (c * 2 + 1 - h, 1 - q)
    fixed_peer = (p, 1 - q)
    right, left = ahead(1), at_chip(c - 1)
    down_a, up_a = pick(even, right, left), pick(even, left, right)
    down_b, up_b = up_a, down_a
    has_up_a = either(odd, c > 0)
    has_down_a = either(even, c > 0)
    has_up_b, has_down_b = has_down_a, has_up_a
    alias_a, alias_b = both(even, c == 0), both(odd, c == 0)
    is_fixed = p == 0

    half_way = chips // 2

    def right_fed(chip):
        return both(chip > half_way, chip < half_way + 3)

    def left_fed(chip):
        return both(chip >= half_way - 3, chip < half_way - 1)

    def fed_a3(to):
        return jnp.where(to[1] == 0, right_fed(to[0] // 2), left_fed(to[0] // 2))

    def fed_b3(to):
        return jnp.where(to[1] == 0, left_fed(to[0] // 2), right_fed(to[0] // 2))

    def fed_b4(to):
        return both(to[1] == 0, to[0] // 2 == chips - 4)

    def home_of(to):
        stays = to[1] == h
        return (jnp.where(stays, to[0], to[0] // 2 * 2 + 1 - h), jnp.where(stays, to[1], 1 - to[1]))

    over = c + 1 >= chips
    partner_right = (jnp.where(over, c, c + 1) * 2 + 1 - h, jnp.where(over, q, 1 - q))
    partner_left = (jnp.maximum(c - 1, 0) * 2 + 1 - h, 1 - q)
    last_a_from, last_b_from = pick(odd, partner_right, partner_left), pick(odd, partner_left, partner_right)
    alias_home = both(odd, c == 0)
    here = (p, q)
    near = both(c >= half_way - 3, c < half_way + 3)
    plain = jnp.logical_not(near)
    send_a2, send_b2 = both(has_down_a, fed_a3(down_a)), both(has_down_b, fed_b3(down_b))
    send_b3 = both(has_down_b, fed_b4(down_b))

    has_b3, has_b4 = either(even, c >= 2), either(even, c >= 1)
    far_to = (
        pick(even, ahead(3), at_chip(jnp.where(c == 0, 2, c - 3))),
        pick(odd, ahead(3), at_chip(jnp.where(c >= 3, c - 3, 3 - c))),
        pick(odd, ahead(4), at_chip(c - 4)),
        at_chip(3 - c),
    )
    first_to_b, second_to_a = alias_b, both(even, c < 3)
    not_fed = (
        jnp.logical_not(jnp.where(first_to_b, fed_b3(far_to[0]), fed_a3(far_to[0]))),
        jnp.logical_not(jnp.where(second_to_a, fed_a3(far_to[1]), fed_b3(far_to[1]))),
        jnp.logical_not(fed_b4(far_to[2])),
    )
    far = (
        (both(either(even, c >= 3, c == 0), not_fed[0]), far_to[0],
         jnp.where(alias_a, B_AT, A_AT), jnp.where(first_to_b, B_AT + 3, A_AT + 3)),
        (both(either(odd, c >= 1), not_fed[1]), far_to[1],
         B_AT, jnp.where(second_to_a, A_AT + 3, B_AT + 3)),
        (both(either(odd, c >= 4), not_fed[2]), far_to[2], B_AT, B_AT + 4),
        (both(odd, c <= 2), far_to[3], A_AT, B_AT + 4),
    )
    from_a3 = (both(has_up_a, jnp.logical_not(fed_a3(here))), pick(even, at_chip(jnp.where(c >= 3, c - 3, 3 - c)), ahead(3)),
               jnp.where(both(even, c < 3), 1, 0))
    from_b3 = (both(has_b3, jnp.logical_not(fed_b3(here))), pick(even, ahead(3), at_chip(jnp.where(c >= 3, c - 3, 2 - c))),
               jnp.where(both(odd, c == 2), 0, 1))
    from_b4 = (both(has_b4, jnp.logical_not(fed_b4(here))), pick(even, ahead(4), at_chip(jnp.where(c >= 4, c - 4, 3 - c))),
               jnp.where(both(odd, c < 4), 3, 2))

    def slot_a(k):
        return jnp.where(alias_a, B_AT + k, A_AT + k)

    def slot_b(k):
        at = jnp.where(both(alias_b, k >= 1), A_AT + k - 1, B_AT + k)
        return jnp.where(both(odd, c == 1, k == 3), A_AT, at)

    def remote(src, dst, send, recv, to):
        return pltpu.make_async_remote_copy(
            src_ref=src, dst_ref=dst, send_sem=send, recv_sem=recv, device_id=to, device_id_type=MESH
        )

    own = pltpu.make_async_copy(factors, mine.at[pl.ds(0, factors.shape[0])], load_sem.at[0])
    swap_in = remote(factors, raw.at[pl.ds(0, factors.shape[0])], in_send, in_recv, partner)

    def counts_in(k):
        return pltpu.make_async_copy(counts.at[2 * k + differs], tiles.at[k], count_sem.at[k])

    def chain_a(k):
        to = A_AT + k + 1
        return remote(x.at[slot_a(k), h], x.at[to, h], out_block_send.at[4 + k], block_recv.at[to], down_a)

    def chain_b(k):
        to = B_AT + k + 1
        return remote(x.at[slot_b(k), h], x.at[to, h], out_block_send.at[7 + k], block_recv.at[to], down_b)

    def far_block(i):
        _, to, at, into = far[i]
        return remote(x.at[at, h], x.at[into, h], out_block_send.at[i], block_recv.at[into], to)

    def arrival(at):
        return remote(x.at[at, h], x.at[at, h], out_block_send.at[0], block_recv.at[at], sibling)

    def to_core(at):
        return remote(x.at[at, h], x.at[at, h], core_send.at[at], core_recv.at[at], sibling)

    def from_core_arrival(at):
        return remote(x.at[at, 1 - h], x.at[at, 1 - h], core_send.at[at], core_recv.at[at], sibling)

    holder = both(other, c >= chips - 4)

    def held(j):
        slot = (jnp.where(odd, A_AT + 1, B_AT + 1), jnp.where(odd, A_AT + 3, B_AT + 3), B_AT + 4)[j]
        chip = (c, 2 * chips - 4 - c, 2 * chips - 5 - c)[j]
        to = (jnp.clip(chip, 0, chips - 1) * 2 + 1 - h, q)
        return remote(spare, x.at[slot, 1 - h], hold_send.at[j], block_recv.at[slot], to)

    holds = (
        both(holder, c == chips - 1),
        both(holder, c >= chips - 3),
        both(holder, even, c <= chips - 2),
    )
    takes_held = (
        (both(same, c >= chips - 3), (jnp.clip(2 * chips - 4 - c, 0, chips - 1) * 2 + 1 - h, q)),
        (both(same, even, c >= chips - 3), (jnp.clip(2 * chips - 5 - c, 0, chips - 1) * 2 + 1 - h, q)),
    )

    def sends(condition, to):
        return both(condition, jnp.logical_not(both(other, to[1] != q)))

    def g_core(at):
        return remote(g.at[at, 1 - h], from_core.at[at], gcore_send.at[at], gcore_recv.at[at], sibling)

    def g_chain(at, to):
        return remote(g.at[at, h], from_chain.at[at - 1], gback_send.at[at], gchain_recv.at[at - 1], to)

    def g_chain_arrival(at):
        return remote(g.at[at, h], from_chain.at[at], gback_send.at[at], gchain_recv.at[at], sibling)

    def g_return(at, source):
        _, to, i = source
        return remote(g.at[at, h], returned.at[i], gback_send.at[at], returned_recv.at[i], to)

    def g_return_arrival(i):
        return remote(g.at[0, h], returned.at[i], gback_send.at[0], returned_recv.at[i], sibling)

    def swap_out(i):
        at = jnp.where(i == 0, A_AT, B_AT)
        return remote(g.at[at, h], swapped.at[i], out_send.at[i], out_recv.at[i], partner)

    fixed_in = remote(x.at[A_AT, 0], x.at[FIXED, 0], fix_send, fix_recv, fixed_peer)
    fixed_out = remote(g.at[FIXED, 1 - q], extra, gfix_send, gfix_recv, fixed_peer)
    fixed_giver = both(is_fixed, even)
    fixed_taker = both(is_fixed, odd)

    def when(condition, action):
        @pl.when(condition)
        def _():
            action()

    share, items = x.shape[2], x.shape[3]
    groups = items // LANES

    def rows_of(block, group):
        return pl.ds(2 * group + block, share, stride=2 * groups)

    def take(source, block, at, half):
        for group in range(groups):
            x[at, half, :, pl.ds(group * LANES, LANES)] = source[rows_of(block, group), :]

    def give(block, value):
        for group in range(groups):
            out[rows_of(block, group), :] = value[:, group * LANES : (group + 1) * LANES]

    when(either(same, fixed_taker, holder), own.start)
    for k in range(4):
        counts_in(k).start()

    barrier = pltpu.get_barrier_semaphore()
    peers = [
        (None, sibling), (None, right), (c > 0, left), (other, partner), (is_fixed, fixed_peer),
        *[(f[0], f[1]) for f in far], from_a3[:2], from_b3[:2], from_b4[:2],
    ]
    greeted = 0
    for condition, to in ((both(other, has_up_a), last_a_from), (both(other, has_up_b), last_b_from)):
        @pl.when(condition)
        def _(to=to):
            pl.semaphore_signal(barrier, inc=1, device_id=to, device_id_type=MESH)

    for condition, to in takes_held:
        @pl.when(condition)
        def _(to=to):
            pl.semaphore_signal(barrier, inc=1, device_id=to, device_id_type=MESH)

    greeted += jnp.where(holds[1], 1, 0) + jnp.where(holds[2], 1, 0)
    for condition, up in ((has_up_a, up_a), (has_up_b, up_b)):
        greeted += jnp.where(both(condition, up[1] != h), 1, 0)
    for condition, to in peers:
        def greet(to=to):
            pl.semaphore_signal(barrier, inc=1, device_id=to, device_id_type=MESH)

        if condition is None:
            greet()
            greeted += 1
        else:
            when(condition, greet)
            greeted += jnp.where(condition, 1, 0)
    pl.semaphore_wait(barrier, greeted)

    when(other, swap_in.start)

    when(either(same, fixed_taker, holder), own.wait)

    @pl.when(holder)
    def _():
        for group in range(groups):
            spare[:, pl.ds(group * LANES, LANES)] = mine[rows_of(0, group), :]
        for j in range(3):
            when(holds[j], held(j).start)

    for source, condition in ((mine, same), (raw, other)):
        @pl.when(condition)
        def _(source=source):
            if source is raw:
                swap_in.wait_recv()
            for block in range(2):
                take(source, block, jnp.where(q == block, A_AT, B_AT), h)

    when(sends(has_down_b, down_b), chain_b(0).start)
    when(sends(has_down_a, down_a), chain_a(0).start)
    to_core(B_AT).start()
    to_core(A_AT).start()
    def crossing(to):
        return (to[0] // 2 >= half_way) != (c >= half_way)

    def send_far(late):
        for i in (1, 0, 2, 3):
            crosses = crossing(far[i][1])
            when(both(sends(*far[i][:2]), crosses if late else jnp.logical_not(crosses)), far_block(i).start)

    send_far(False)
    when(fixed_giver, fixed_in.start)

    @pl.loop(0, SLOTS)
    def _(at):
        g[at] = jnp.zeros_like(g[at])

    padded = upper_parts.shape[0] // 4
    if padded > share:
        for parts in (upper_parts, lower_parts):
            for i in range(4):
                parts[pl.ds(i * padded + share, padded - share), :] = jnp.zeros((padded - share, items), BF16)

    @pl.when(fixed_taker)
    def _():
        take(mine, 0, FIXED, 1)
        fixed_in.wait_recv()

    def meeting(k):
        a, b = slot_a(k), slot_b(k + differs)
        upper = jnp.where(is_fixed, jnp.where(even, A_AT, FIXED), jnp.where(even, a, b))
        lower = jnp.where(even, b, a)
        g_upper = jnp.where(is_fixed, FIXED, upper)
        counts_in(k).wait()
        for parts, at in ((upper_parts, upper), (lower_parts, lower)):
            for half in range(2):
                high, low = split(x[at, half])
                parts[pl.ds(half * padded, share), :] = high
                parts[pl.ds((2 + half) * padded, share), :] = low
        lower_twice[: 2 * padded] = lower_parts[: 2 * padded]
        lower_twice[2 * padded :] = lower_parts[: 2 * padded]
        over_features = ((0,), (0,))
        scores = product(upper_parts[...], lower_twice[...], over_features) + product(
            upper_parts[: 2 * padded], lower_parts[2 * padded :], over_features
        )
        r_high, r_low = split(residual_of(scores, tiles[k]))

        def add_to(at, parts, dims):
            first = product(parts[...], r_high, dims)
            second = product(parts[: 2 * padded], r_low, dims)
            for half in range(2):
                i, j = half * padded, (2 + half) * padded
                g[at, half] += first[i : i + share] + first[j : j + share] + second[i : i + share]

        add_to(lower, upper_parts, ((1,), (0,)))
        add_to(g_upper, lower_parts, ((1,), (1,)))

    has = {1: has_up_a, 2: has_up_a, 3: has_up_a, 5: has_up_b, 6: has_up_b, 7: has_b3, 8: has_b4}

    def pass_on(at, copy=None, condition=None):
        when(has[at], arrival(at).wait_recv)
        if copy is not None:
            when(condition, copy.start)
        when(has[at], to_core(at).start)

    def second_blocks():
        pass_on(B_AT + 2, chain_b(2), send_b2)
        pass_on(A_AT + 2, chain_a(2), send_a2)

    def far_blocks():
        pass_on(B_AT + 3, chain_b(3), send_b3)
        pass_on(A_AT + 3)
        pass_on(B_AT + 4)

    def other_half(at, condition=None):
        conditions = [i for i in (has.get(at), condition) if i is not None]
        if conditions:
            when(both(*conditions), from_core_arrival(at).wait_recv)
        else:
            from_core_arrival(at).wait_recv()

    def gathered(at):
        g_core(at).wait_recv()
        g[at, h] += from_core[at]

    def give_back(at, source, present, up):
        when(source[0], g_return(at, source).start)
        when(both(present, jnp.logical_not(source[0])), g_chain(at, up).start)

    def far_back():
        g_core(B_AT + 4).start()
        g_core(A_AT + 3).start()
        g_core(B_AT + 3).start()
        gathered(B_AT + 4)
        give_back(B_AT + 4, from_b4, has_b4, up_b)
        gathered(A_AT + 3)
        give_back(A_AT + 3, from_a3, has_up_a, up_a)
        gathered(B_AT + 3)

        @pl.when(send_b3)
        def _():
            g_chain_arrival(B_AT + 3).wait_recv()
            g[B_AT + 3, h] += from_chain[B_AT + 3]

        give_back(B_AT + 3, from_b3, has_b3, up_b)

    def in_turn(*ks):
        turn_at = ks[-1]
        for i in range(len(ks) - 2, -1, -1):
            turn_at = jnp.where(turn_now[0] == i, ks[i], turn_at)
        return turn_at

    near_same, near_other = both(near, same), both(near, other)
    plain_same, plain_other = both(plain, same), both(plain, other)
    turn_now = [0]
    order = (
        0,
        jnp.where(plain_other, 3, 1),
        jnp.where(plain_same, 3, 2),
        jnp.where(near, 3, jnp.where(same, 2, 1)),
    )

    @pl.loop(0, 4)
    def _(turn):
        turn_now[0] = turn

        @pl.when(turn == 0)
        def _():
            pass_on(B_AT + 1, chain_b(1), has_down_b)
            pass_on(A_AT + 1, chain_a(1), has_down_a)
            other_half(B_AT)
            other_half(A_AT)
            send_far(True)
            other_half(B_AT + 1, other)

        @pl.when(turn == 1)
        def _():
            when(near, second_blocks)
            when(plain, far_blocks)
            other_half(A_AT + 1, either(same, near))
            other_half(B_AT + 1, same)
            other_half(B_AT + 2, near_other)
            other_half(A_AT + 3, plain_other)
            other_half(B_AT + 3, plain_other)
            other_half(B_AT + 4, plain_other)

        @pl.when(turn == 2)
        def _():
            when(near, far_blocks)
            when(plain, second_blocks)
            other_half(A_AT + 3, plain_same)
            other_half(B_AT + 3, either(plain_same, near_other))
            other_half(A_AT + 2, either(other, alias_b, near))
            other_half(B_AT + 2, either(plain_other, near_same))

        @pl.when(turn == 3)
        def _():
            when(plain, far_back)
            other_half(A_AT + 1, plain_other)
            other_half(A_AT + 2, both(plain_same, jnp.logical_not(alias_b)))
            other_half(B_AT + 2, plain_same)
            other_half(A_AT + 3, near)
            other_half(B_AT + 3, near_same)
            other_half(B_AT + 4, near_other)

        meeting(in_turn(*order))

    when(near, far_back)
    for k in (2, 1, 0):
        g_core(A_AT + k).start()
        g_core(B_AT + k).start()
    when(is_fixed, fixed_out.start)

    def chained(at, alias, has_down):
        @pl.when(has_down)
        def _():
            g_chain_arrival(at).wait_recv()
            g[alias, h] += from_chain[at]

    def add_returned(i, at):
        @pl.when(far[i][0])
        def _():
            g_return_arrival(i).wait_recv()
            g[at, h] += returned[i]

    gathered(A_AT + 2)
    chained(A_AT + 2, slot_a(2), send_a2)
    when(has_up_a, g_chain(A_AT + 2, up_a).start)
    gathered(B_AT + 2)
    chained(B_AT + 2, slot_b(2), send_b2)
    when(has_up_b, g_chain(B_AT + 2, up_b).start)
    gathered(A_AT)
    gathered(B_AT)
    chained(B_AT + 1, slot_b(1), alias_b)
    for i in (0, 1, 2, 3):
        add_returned(i, far[i][2])

    @pl.when(other)
    def _():
        swap_out(0).start()
        swap_out(1).start()

    gathered(A_AT + 1)
    gathered(B_AT + 1)
    chained(A_AT + 1, slot_a(1), has_down_a)
    when(has_up_a, g_chain(A_AT + 1, home_of(up_a)).start)
    chained(B_AT + 1, B_AT + 1, both(has_down_b, jnp.logical_not(alias_b)))
    when(has_up_b, g_chain(B_AT + 1, home_of(up_b)).start)
    @pl.when(other)
    def _():
        swap_out(0).wait_recv()
        swap_out(1).wait_recv()

        @pl.when(has_up_a)
        def _():
            g_chain_arrival(A_AT).wait_recv()
            swapped[jnp.where(alias_home, 1, 0)] += from_chain[A_AT]

        for block in range(2):
            when(q == 1 - block, functools.partial(lambda b: give(b, swapped[0]), block))

        @pl.when(has_up_b)
        def _():
            g_chain_arrival(B_AT).wait_recv()
            swapped[1] += from_chain[B_AT]

        for block in range(2):
            when(q == block, functools.partial(lambda b: give(b, swapped[1]), block))

    @pl.when(same)
    def _():
        chained(A_AT, slot_a(0), has_down_a)
        for block in range(2):
            when(q == block, functools.partial(lambda b: give(b, g[A_AT, h]), block))
        chained(B_AT, B_AT, has_down_b)
        for block in range(2):
            when(q == 1 - block, functools.partial(lambda b: give(b, g[B_AT, h]), block))

    @pl.when(is_fixed)
    def _():
        fixed_out.wait_recv()
        for group in range(groups):
            lanes = pl.ds(group * LANES, LANES)
            out[rows_of(0, group), :] += g[FIXED, q, :, lanes] + extra[:, lanes]

    other_half(B_AT + 4, same)

    @pl.when(other)
    def _():
        swap_in.wait_send()
        swap_out(0).wait_send()
        swap_out(1).wait_send()

    when(fixed_giver, fixed_in.wait_send)
    for j in range(3):
        when(holds[j], held(j).wait_send)
    when(is_fixed, fixed_out.wait_send)
    for i in range(4):
        when(sends(*far[i][:2]), far_block(i).wait_send)
    for k in range(2):
        when(sends(has_down_a, down_a) if k == 0 else has_down_a, chain_a(k).wait_send)
        when(sends(has_down_b, down_b) if k == 0 else has_down_b, chain_b(k).wait_send)
    when(send_a2, chain_a(2).wait_send)
    when(send_b2, chain_b(2).wait_send)
    when(send_b3, chain_b(3).wait_send)
    for at in range(9):
        if at in has:
            when(has[at], to_core(at).wait_send)
        else:
            to_core(at).wait_send()
        g_core(at).wait_send()
    for k in (1, 2):
        when(has_up_a, g_chain(A_AT + k, home_of(up_a) if k == 1 else up_a).wait_send)
        when(has_up_b, g_chain(B_AT + k, home_of(up_b) if k == 1 else up_b).wait_send)
    for at, source, present, up in (
        (A_AT + 3, from_a3, has_up_a, up_a), (B_AT + 3, from_b3, has_b3, up_b), (B_AT + 4, from_b4, has_b4, up_b),
    ):
        when(source[0], g_return(at, source).wait_send)
        when(both(present, jnp.logical_not(source[0])), g_chain(at, up).wait_send)


def solution(mesh):
    players = mesh.shape["blk"]
    chips = players // 2

    def body(factors, state, counts):
        share, items = factors.shape[2], factors.shape[3]
        padded = -(-share // 16) * 16
        dma = pltpu.SemaphoreType.DMA
        packed = pack(factors[0])
        room = -(-share // 8) * 8 * 2 * items // LANES
        grad = pl.pallas_call(
            functools.partial(kernel, chips),
            out_shape=jax.ShapeDtypeStruct((room, LANES), F32),
            in_specs=[pl.BlockSpec(memory_space=pl.ANY)] * 2,
            out_specs=pl.BlockSpec(memory_space=pltpu.VMEM),
            scratch_shapes=[
                pltpu.VMEM((SLOTS, 2, share, items), F32),
                pltpu.VMEM((SLOTS, 2, share, items), F32),
                pltpu.VMEM((room, LANES), F32),
                pltpu.VMEM((room, LANES), F32),
                pltpu.VMEM((share, items), F32),
                pltpu.VMEM((9, share, items), F32),
                pltpu.VMEM((8, share, items), F32),
                pltpu.VMEM((4, share, items), F32),
                pltpu.VMEM((2, share, items), F32),
                pltpu.VMEM((share, items), F32),
                pltpu.VMEM((4, items, items), jnp.int32),
                pltpu.VMEM((4 * padded, items), BF16),
                pltpu.VMEM((4 * padded, items), BF16),
                pltpu.VMEM((4 * padded, items), BF16),
                dma((2,)), dma((4,)),
                dma, dma, dma, dma, dma((3,)),
                dma((11,)), dma((9,)), dma((9,)), dma((9,)),
                dma((9,)), dma((9,)), dma((9,)), dma((8,)), dma((4,)),
                dma((2,)), dma((2,)), dma, dma,
            ],
            compiler_params=pltpu.CompilerParams(
                collective_id=0, has_side_effects=True, vmem_limit_bytes=60 * 1024 * 1024
            ),
        )(packed, counts[0])
        grad = grad[: packed.shape[0]]
        new_state = pack(state[0]) + grad * grad
        step = grad / jnp.sqrt(new_state)
        return (unpack(step, factors.shape), unpack(new_state, factors.shape))

    in_specs = (
        P("blk", None, "rep", None),
        P("blk", None, "rep", None),
        P("blk", None, None, None),
    )
    out_specs = (P("blk", None, "rep", None), P("blk", None, "rep", None))
    return jax.shard_map(body, mesh=mesh, in_specs=in_specs, out_specs=out_specs, check_vma=False)
```
